256 devices in a mesh: row: 16 (over x, z_hi), col: 8 (over y, core), seq: 2 (over z_lo).
Axes of the slice: x: 4, y: 4, z: 8 (z_hi: 4, z_lo: 2; z = z_hi * 2 + z_lo), core: 2. Of those that a mesh axis runs over, the one named last changes fastest.
Arguments:
- out_grads: bfloat16 [1, 2048, 32768], P(None, 'seq', 'row'), may hold values from -0.125 to 0.125
- layer_inputs: bfloat16 [1, 2048, 8192], P(None, 'seq', 'col'), may hold values from -6 to 6
- row_bits: int32 [32768], P('row'), may hold values from 0 to 1
- col_bits: int32 [8192], P('col'), may hold values from 0 to 1
- row_blocks: int32 [16], replicated, may hold values from 0 to 511
- col_blocks: int32 [8], replicated, may hold values from 0 to 63
Outputs:
- sketch: float32 [1, 1024, 1024], P(None, 'row', 'col')
The draws below stay inside these ranges and needn't reach their ends.
Inputs may be any that keep to these rules, and one draw needn't show every extreme that they name: `row_blocks`: blocks may repeat. `col_blocks`: blocks may repeat.
All inputs are finite; a program needn't handle non-finite values.
Results may differ from the reference program's by a relative error of at most 0.0003.
Values sent between devices are 32-bit elements; how exact they have to be, the bound alone decides.
A program may use at most 64 MiB of HBM per device.

```python
import math
import jax
import jax.numpy as jnp
from jax import lax

D = 8192
FF = 28672
FFP = 32768
EX = 1
TOKENS = 2048
BR = 64
KR = 16
BC = 128
KC = 8


def touch_ends(entries, stream_key, smallest, largest):
    extent = entries.shape
    index_at = [jax.random.randint(jax.random.fold_in(stream_key, axis), (), 0, extent[axis]) for axis in range(len(extent))]
    entries = entries.at[tuple(index_at)].set(smallest)
    longest = extent.index(max(extent))
    index_at[longest] = (index_at[longest] + 1) % extent[longest]
    return entries.at[tuple(index_at)].set(largest)


def shard_levels(stream_key, shape, split, least, top_value):
    factor_of, own = 1.0, jax.random.fold_in(stream_key, 6)
    for axis_at, blocks in split:
        steps = jnp.exp(jax.random.uniform(jax.random.fold_in(own, axis_at), (blocks,), jnp.float32, least / len(split), top_value / len(split)))
        factor_of = factor_of * jnp.repeat(steps, shape[axis_at] // blocks).reshape([-1 if axis == axis_at else 1 for axis in range(len(shape))])
    return factor_of


def gaussian(own_key, shape, spread, most, pieces=(), kind=jnp.bfloat16):
    array = spread * jax.random.normal(own_key, shape, jnp.float32)
    if pieces:
        array = array * shard_levels(own_key, shape, pieces, -0.22, 0.18)
    return jnp.clip(array, -most, most).astype(kind)


def setup_inputs(seed: int = 0) -> dict:
    splits = jax.random.split(jax.random.key(seed), 7)
    out_grads = gaussian(splits[0], (EX, TOKENS, FFP), (TOKENS ** -0.5), 0.125, ((1, 2), (2, 16)))
    layer_inputs = gaussian(splits[1], (EX, TOKENS, D), 1.0, 6.0, ((1, 2), (2, 8)))
    row_bits = touch_ends(jax.random.randint(splits[2], (FFP,), 0, 2), jax.random.fold_in(splits[2], 1), 0, 1).astype(jnp.int32)
    col_bits = touch_ends(jax.random.randint(splits[3], (D,), 0, 2), jax.random.fold_in(splits[3], 1), 0, 1).astype(jnp.int32)
    row_blocks = touch_ends(jax.random.randint(splits[4], (KR,), 0, FFP // BR), jax.random.fold_in(splits[4], 1), 0, (FFP // BR) - 1).astype(jnp.int32)
    col_blocks = touch_ends(jax.random.randint(splits[5], (KC,), 0, D // BC), jax.random.fold_in(splits[5], 1), 0, (D // BC) - 1).astype(jnp.int32)
    return {"out_grads": out_grads, "layer_inputs": layer_inputs, "row_bits": row_bits, "col_bits": col_bits, "row_blocks": row_blocks, "col_blocks": col_blocks}


def parity_sign(first, second):
    joined = jnp.bitwise_and(first, second)
    parity = jnp.zeros(joined.shape, jnp.int32)
    for position in range(16):
        parity = parity + jnp.bitwise_and(jnp.right_shift(joined, position), 1)
    return (1 - 2 * (parity % 2)).astype(jnp.float32)

def hadamard_table(order):
    index = jnp.arange(order, dtype=jnp.int32)
    return parity_sign(index[:, None], index[None, :])

def mix_last(values):
    length = values.shape[-1]
    batch = math.prod(values.shape[:-1])
    mixing = values.reshape(batch, length)
    before = 1
    remaining = length
    while remaining > 1:
        factor = min(64, remaining)
        after = remaining // factor
        table = hadamard_table(factor)
        mixing = jnp.einsum('ij,bpjq->bpiq', table, mixing.reshape(batch, before, factor, after), precision=lax.Precision.HIGHEST)
        before = before * factor
        remaining = after
    return mixing.reshape(values.shape)

def reference(out_grads, layer_inputs, row_bits, col_bits, row_blocks, col_blocks):
    row_sign = (1 - 2 * row_bits).astype(jnp.float32) * (jnp.arange(FFP, dtype=jnp.int32) < FF).astype(jnp.float32)
    col_sign = (1 - 2 * col_bits).astype(jnp.float32)
    left = mix_last(out_grads.astype(jnp.float32) * row_sign)
    left = jnp.take(left.reshape(EX, TOKENS, FFP // BR, BR), row_blocks, axis=2).reshape(EX, TOKENS, KR * BR)
    right = mix_last(layer_inputs.astype(jnp.float32) * col_sign)
    right = jnp.take(right.reshape(EX, TOKENS, D // BC, BC), col_blocks, axis=2).reshape(EX, TOKENS, KC * BC)
    sketch = jnp.einsum('etk,etj->ekj', left, right, precision=lax.Precision.HIGHEST)
    return sketch / math.sqrt(FFP * D)
```

```python
import math

import jax
import jax.numpy as jnp
from jax import lax
from jax.experimental import pallas as pl
from jax.experimental.pallas import tpu as pltpu
from jax.sharding import PartitionSpec as P

D = 8192
FF = 28672
FFP = 32768
SCALE = 1.0 / math.sqrt(FFP * D)
MESH = pl.DeviceIdType.MESH
CHUNKS = 4
F32 = jnp.float32
BF16 = jnp.bfloat16


def parity(value):
    value = value ^ (value >> 4)
    value = value ^ (value >> 2)
    value = value ^ (value >> 1)
    return value & 1


def butterfly(parts):
    stride = 1
    while stride < len(parts):
        for at in range(len(parts)):
            if not at & stride:
                low, high = parts[at], parts[at + stride]
                parts[at], parts[at + stride] = low + high, low - high
        stride *= 2
    return parts


def split(value):
    high = value.astype(BF16)
    return high, (value - high.astype(F32)).astype(BF16)


def kernel(
    row_blocks, col_blocks, row_bits, col_bits, grads, inputs, out,
    xbuf, ybuf, hmat, rmix, cmix, asend, xrecv, asum, zrecv, aall,
    bsend, brecv, ball, psend, precv,
    load_x, load_y, xs, xr, zs, zr, ys, yr, b1s, b1r, b2s, b2r, b3s, b3r, ps, pr,
):
    row, col, seq = lax.axis_index("row"), lax.axis_index("col"), lax.axis_index("seq")
    x, zh = row // 4, row % 4
    y, core = col // 2, col % 2

    loads_y = []
    for half in range(2):
        start = pl.multiple_of((x * 2 + half) * 128 + zh * 32, 32)
        loads_y.append(
            pltpu.make_async_copy(inputs.at[0, pl.ds(start, 32)], ybuf.at[half], load_y.at[half])
        )
    loads_x = []
    for chunk in range(CHUNKS):
        start = pl.multiple_of(col * 128 + chunk * 32, 32)
        loads_x.append(
            pltpu.make_async_copy(grads.at[0, pl.ds(start, 32)], xbuf.at[chunk], load_x.at[chunk])
        )
    for load in loads_y + loads_x:
        load.start()

    def at_x(step):
        return {"row": ((x + step) % 4) * 4 + zh}

    def at_zh(step):
        return {"row": x * 4 + (zh + step) % 4}

    def at_col(dy, dc):
        return {"col": ((y + dy) % 4) * 2 + (core + dc) % 2}

    def at_seq(ds, dc):
        return {"seq": (seq + ds) % 2, "col": y * 2 + (core + dc) % 2}

    barrier = pltpu.get_barrier_semaphore()
    partners = [at_x(step) for step in (1, 2, 3)] + [at_zh(step) for step in (1, 2, 3)]
    partners += [at_col(dy, dc) for dy in range(4) for dc in range(2) if dy + dc]
    partners += [at_seq(1, 0), at_seq(1, 1)]
    for partner in partners:
        pl.semaphore_signal(barrier, inc=1, device_id=partner, device_id_type=MESH)

    sends = []

    def send(src, dst, send_sem, recv_sem, device):
        copy = pltpu.make_async_remote_copy(
            src_ref=src, dst_ref=dst, send_sem=send_sem, recv_sem=recv_sem,
            device_id=device, device_id_type=MESH,
        )
        copy.start()
        sends.append(copy)
        return copy

    first = lax.broadcasted_iota(jnp.int32, (256, 256), 0)
    second = lax.broadcasted_iota(jnp.int32, (256, 256), 1)
    hmat[...] = (1 - 2 * parity(first & second)).astype(F32).astype(BF16)
    place = lax.broadcasted_iota(jnp.int32, (16, 128), 0) * 128
    place = place + lax.broadcasted_iota(jnp.int32, (16, 128), 1) + row * 2048
    row_sign = jnp.where(place < FF, (1 - 2 * row_bits[...]).astype(F32), 0.0).astype(BF16)
    col_sign = (1 - 2 * col_bits[...]).astype(F32).astype(BF16)
    lane_high = lax.broadcasted_iota(jnp.int32, (16, 128), 1) // 64
    low = lane_high == 0

    for load in loads_y:
        load.wait()
    tiles = []
    for half in range(2):
        for group in range(4):
            sign = jnp.concatenate(
                [col_sign[2 * group : 2 * group + 1], col_sign[2 * group + 1 : 2 * group + 2]], axis=1
            )
            tiles.append(ybuf[half, :, group * 256 : (group + 1) * 256] * sign)
    mixed = jnp.dot(jnp.concatenate(tiles, axis=0), hmat[...], preferred_element_type=F32)
    for half in range(2):
        for tile in range(2):
            parts = butterfly([
                mixed[(half * 4 + g) * 32 : (half * 4 + g + 1) * 32, tile * 128 : (tile + 1) * 128]
                for g in range(4)
            ])
            for g in range(4):
                cmix[g * 2 + tile, half * 32 : (half + 1) * 32] = parts[g]
    for m in range(8):
        block = col_blocks[m]
        sign = (1 - 2 * parity((block // 8) & col)).astype(F32)
        kept = cmix[block % 8] * sign
        for half in range(2):
            bsend[(m // 2) * 2 + half, m % 2] = kept[half * 32 : (half + 1) * 32]

    pl.semaphore_wait(barrier, len(partners))

    b1 = []
    for dy in (2, 1, 3, 0):
        for dc in range(2):
            if dy + dc:
                j = dy * 2 + dc - 1
                target = ((y + dy) % 4) * 2 + (core + dc) % 2
                b1.append(send(bsend.at[target], brecv.at[j], b1s.at[j], b1r.at[j], at_col(dy, dc)))

    to_x = []
    for chunk in range(CHUNKS):
        loads_x[chunk].wait()
        tiles = []
        for group in range(8):
            sign = jnp.concatenate(
                [row_sign[2 * group : 2 * group + 1], row_sign[2 * group + 1 : 2 * group + 2]], axis=1
            )
            tiles.append(xbuf[chunk, :, group * 256 : (group + 1) * 256] * sign)
        mixed = jnp.dot(jnp.concatenate(tiles, axis=0), hmat[...], preferred_element_type=F32)
        for tile in range(2):
            parts = butterfly(
                [mixed[g * 32 : (g + 1) * 32, tile * 128 : (tile + 1) * 128] for g in range(8)]
            )
            for g in range(8):
                rmix[g * 2 + tile] = parts[g]
        for k in range(16):
            block = row_blocks[k]
            sign = (1 - 2 * parity((block // 32) & row)).astype(F32) * SCALE
            kept = rmix[(block % 32) // 2]
            above, below = kept[:16], kept[16:]
            straight = jnp.where(low, above, below)
            crossed = pltpu.roll(jnp.where(low, below, above), 64, 1)
            asend[chunk, k] = jnp.where((lane_high ^ (block % 2)) == 0, straight, crossed) * sign
        copies = []
        for step in (2, 1, 3):
            first_k = ((x + step) % 4) * 4
            copies.append(send(
                asend.at[chunk, pl.ds(first_k, 4)], xrecv.at[chunk, step - 1],
                xs.at[chunk, step - 1], xr.at[chunk, step - 1], at_x(step),
            ))
        to_x.append(copies)

    to_zh = []

    def reduce_x(chunk):
        for copy in to_x[chunk]:
            copy.wait_recv()
        own = asend[chunk, pl.ds(x * 4, 4)]
        asum[chunk] = (own + xrecv[chunk, 0]) + (xrecv[chunk, 1] + xrecv[chunk, 2])
        to_zh.append([
            send(asum.at[chunk, (zh + step) % 4], zrecv.at[chunk, step - 1],
                 zs.at[chunk, step - 1], zr.at[chunk, step - 1], at_zh(step))
            for step in (2, 1, 3)
        ])

    to_y = []

    def reduce_zh(chunk):
        for copy in to_zh[chunk]:
            copy.wait_recv()
        aall[y, chunk] = (asum[chunk, zh] + zrecv[chunk, 0]) + (zrecv[chunk, 1] + zrecv[chunk, 2])
        to_y.append([
            send(aall.at[y, chunk], aall.at[y, chunk], ys.at[chunk, step - 1], yr.at[chunk, step - 1],
                 at_col(step, 0))
            for step in (2, 1, 3)
        ])

    b3 = []

    def forward(j):
        block = (zh + 4 - j) % 4
        for step in (2, 1, 3):
            b3.append(send(ball.at[x, block], ball.at[x, block], b3s.at[j, step - 1], b3r.at[j, step - 1],
                           at_x(step)))

    reduce_x(0)

    for copy in b1:
        copy.wait_recv()
    total = bsend[col]
    for j in range(7):
        total = total + brecv[j]
    ball[x, zh] = total
    b2 = {
        step: send(ball.at[x, zh], ball.at[x, zh], b2s.at[step - 1], b2r.at[step - 1], at_zh(step))
        for step in (2, 1, 3)
    }
    for chunk in range(1, CHUNKS):
        reduce_x(chunk)
    forward(0)
    for step in (1, 3):
        b2[step].wait_recv()
        forward(step)
    reduce_zh(0)
    b2[2].wait_recv()
    forward(2)
    for chunk in range(1, CHUNKS):
        reduce_zh(chunk)

    for copy in b3:
        copy.wait_recv()
    for copies in to_y:
        for copy in copies:
            copy.wait_recv()
    left_high, left_low = split(aall[...].reshape(256, 128))
    halves = []
    for half in range(2):
        right = jnp.concatenate(
            [ball[:, :, m, half * 16 : (half + 1) * 16, :].reshape(256, 128) for m in range(2)], axis=1
        )
        right_high, right_low = split(right)

        def product(first, second):
            return lax.dot_general(first, second, (((0,), (0,)), ((), ())), preferred_element_type=F32)

        full = (
            product(left_high, right_high)
            + product(left_high, right_low)
            + product(left_low, right_high)
        )
        halves.append(full[half * 64 : (half + 1) * 64])
    partial = halves[0] + halves[1]
    psend[0] = partial[:, :128]
    psend[1] = partial[:, 128:]
    mine = seq * 2 + core
    last = []
    for j, (ds, dc) in enumerate(((1, 0), (1, 1), (0, 1))):
        last.append(send(psend.at[(core + dc) % 2], precv.at[mine], ps.at[j], pr.at[j], at_seq(ds, dc)))
    precv[mine] = psend[core]
    for copy in last:
        copy.wait_recv()
    out[0] = (precv[0] + precv[1]) + (precv[2] + precv[3])
    for copy in sends:
        copy.wait_send()


def body(out_grads, layer_inputs, row_bits, col_bits, row_blocks, col_blocks):
    vmem = pl.BlockSpec(memory_space=pltpu.VMEM)
    smem = pl.BlockSpec(memory_space=pltpu.SMEM)
    hbm = pl.BlockSpec(memory_space=pl.ANY)
    dma = pltpu.SemaphoreType.DMA
    return pl.pallas_call(
        kernel,
        out_shape=jax.ShapeDtypeStruct((1, 64, 128), F32),
        in_specs=[smem, smem, vmem, vmem, hbm, hbm],
        out_specs=vmem,
        scratch_shapes=[
            pltpu.VMEM((CHUNKS, 32, 2048), BF16),
            pltpu.VMEM((2, 32, 1024), BF16),
            pltpu.VMEM((256, 256), BF16),
            pltpu.VMEM((16, 32, 128), F32),
            pltpu.VMEM((8, 64, 128), F32),
            pltpu.VMEM((CHUNKS, 16, 16, 128), F32),
            pltpu.VMEM((CHUNKS, 3, 4, 16, 128), F32),
            pltpu.VMEM((CHUNKS, 4, 16, 128), F32),
            pltpu.VMEM((CHUNKS, 3, 16, 128), F32),
            pltpu.VMEM((4, CHUNKS, 16, 128), F32),
            pltpu.VMEM((8, 2, 32, 128), F32),
            pltpu.VMEM((7, 2, 32, 128), F32),
            pltpu.VMEM((4, 4, 2, 32, 128), F32),
            pltpu.VMEM((2, 64, 128), F32),
            pltpu.VMEM((4, 64, 128), F32),
            dma((CHUNKS,)),
            dma((2,)),
            dma((CHUNKS, 3)), dma((CHUNKS, 3)),
            dma((CHUNKS, 3)), dma((CHUNKS, 3)),
            dma((CHUNKS, 3)), dma((CHUNKS, 3)),
            dma((7,)), dma((7,)),
            dma((3,)), dma((3,)),
            dma((4, 3)), dma((4, 3)),
            dma((3,)), dma((3,)),
        ],
        compiler_params=pltpu.CompilerParams(collective_id=0, has_side_effects=True),
        name="sketch",
    )(
        row_blocks, col_blocks, row_bits.reshape(16, 128), col_bits.reshape(8, 128),
        out_grads, layer_inputs,
    )


def solution(mesh):
    in_specs = (P(None, "seq", "row"), P(None, "seq", "col"), P("row"), P("col"), P(), P())
    out_specs = P(None, "row", "col")
    return jax.shard_map(body, mesh=mesh, in_specs=in_specs, out_specs=out_specs, check_vma=False)
```

```python
import math

import jax
import jax.numpy as jnp
from jax import lax
from jax.experimental import pallas as pl
from jax.experimental.pallas import tpu as pltpu
from jax.sharding import PartitionSpec as P

D = 8192
FF = 28672
FFP = 32768
SCALE = 1.0 / math.sqrt(FFP * D)
MESH = pl.DeviceIdType.MESH
CHUNKS = 4
F32 = jnp.float32
BF16 = jnp.bfloat16


def parity(value):
    value = value ^ (value >> 4)
    value = value ^ (value >> 2)
    value = value ^ (value >> 1)
    return value & 1


def butterfly(parts):
    stride = 1
    while stride < len(parts):
        for at in range(len(parts)):
            if not at & stride:
                low, high = parts[at], parts[at + stride]
                parts[at], parts[at + stride] = low + high, low - high
        stride *= 2
    return parts


def split(value):
    high = value.astype(BF16)
    return high, (value - high.astype(F32)).astype(BF16)


def kernel(
    row_blocks_in, col_blocks_in, row_bits_in, col_bits_in, grads, inputs, out,
    row_blocks, col_blocks, row_bits, col_bits,
    xbuf, ybuf, hmat, rmix, cmix, asend, xrecv, asum, zrecv, aall,
    bsend, bpair, bsum, brecv, ball, psend, precv,
    load_x, load_y, load_s, xs, xr, zs, zr, ys, yr, b1s, b1r, b2s, b2r, b3s, b3r, ps, pr,
):
    row, col, seq = lax.axis_index("row"), lax.axis_index("col"), lax.axis_index("seq")
    x, zh = row // 4, row % 4
    y, core = col // 2, col % 2

    def at_x(step):
        return {"row": ((x + step) % 4) * 4 + zh}

    def at_zh(step):
        return {"row": x * 4 + (zh + step) % 4}

    def at_col(dy, dc):
        return {"col": ((y + dy) % 4) * 2 + (core + dc) % 2}

    other_seq = {"seq": 1 - seq}
    around = [(dy, dc) for dy in (2, 1, 3, 0) for dc in range(2) if dy + dc]

    barrier = pltpu.get_barrier_semaphore()
    partners = [at_x(step) for step in (2, 1, 3)] + [at_zh(step) for step in (2, 1, 3)]
    partners += [at_col(dy, dc) for dy, dc in around] + [other_seq]
    for partner in partners:
        pl.semaphore_signal(barrier, inc=1, device_id=partner, device_id_type=MESH)

    small = [
        pltpu.make_async_copy(src, dst, load_s.at[at])
        for at, (src, dst) in enumerate((
            (row_bits_in, row_bits), (row_blocks_in, row_blocks),
            (col_bits_in, col_bits), (col_blocks_in, col_blocks),
        ))
    ]
    loads_x = []
    for chunk in range(CHUNKS):
        start = pl.multiple_of(col * 128 + chunk * 32, 32)
        loads_x.append(
            pltpu.make_async_copy(grads.at[0, pl.ds(start, 32)], xbuf.at[chunk], load_x.at[chunk])
        )
    loads_y = [
        pltpu.make_async_copy(
            inputs.at[0, pl.ds(pl.multiple_of((x * 2 + half) * 128 + chunk * 32, 32), 32)],
            ybuf.at[chunk, half], load_y.at[chunk],
        )
        for chunk in range(CHUNKS)
        for half in range(2)
    ]
    for load in small[:2] + loads_x[:1] + small[2:] + loads_y[:2] + loads_x[1:] + loads_y[2:]:
        load.start()

    def send(src, dst, send_sem, recv_sem, device):
        pltpu.make_async_remote_copy(
            src_ref=src, dst_ref=dst, send_sem=send_sem, recv_sem=recv_sem,
            device_id=device, device_id_type=MESH,
        ).start()

    def arrived(ref, sem):
        pltpu.make_async_copy(ref, ref, sem).wait()

    first = lax.broadcasted_iota(jnp.int32, (256, 256), 0)
    second = lax.broadcasted_iota(jnp.int32, (256, 256), 1)
    hmat[...] = (1 - 2 * parity(first & second)).astype(F32).astype(BF16)
    lane_high = lax.broadcasted_iota(jnp.int32, (16, 128), 1) // 64
    low = lane_high == 0
    place = lax.broadcasted_iota(jnp.int32, (16, 128), 0) * 128
    place = place + lax.broadcasted_iota(jnp.int32, (16, 128), 1) + row * 2048
    for load in small[:2]:
        load.wait()
    row_sign = jnp.where(place < FF, (1 - 2 * row_bits[...]).astype(F32), 0.0).astype(BF16)

    def mix_columns(chunk):
        arrived(ybuf.at[chunk], load_y.at[chunk])
        tiles = []
        for half in range(2):
            for group in range(4):
                sign = jnp.concatenate(
                    [col_sign[2 * group : 2 * group + 1], col_sign[2 * group + 1 : 2 * group + 2]], axis=1
                )
                tiles.append(ybuf[chunk, half, :, group * 256 : (group + 1) * 256] * sign)
        mixed = jnp.dot(jnp.concatenate(tiles, axis=0), hmat[...], preferred_element_type=F32)
        for half in range(2):
            for tile in range(2):
                parts = butterfly([
                    mixed[(half * 4 + g) * 32 : (half * 4 + g + 1) * 32, tile * 128 : (tile + 1) * 128]
                    for g in range(4)
                ])
                for g in range(4):
                    cmix[g * 2 + tile, half * 32 : (half + 1) * 32] = parts[g]
        for m in range(8):
            block = col_blocks[m]
            sign = (1 - 2 * parity((block // 8) & col)).astype(F32)
            kept = cmix[block % 8] * sign
            bsend[chunk, m % 2, m // 2] = kept.reshape(2, 32, 128)
        send(bsend.at[chunk, 1 - core], bpair.at[chunk], b1s, b1r.at[chunk], at_col(0, 1))

    def pair_columns(chunk):
        arrived(bpair.at[chunk], b1r.at[chunk])
        bsum[chunk] = bsend[chunk, core] + bpair[chunk]
        for step in (2, 1, 3):
            send(bsum.at[chunk, (y + step) % 4], brecv.at[chunk, step - 1], b2s, b2r.at[chunk], at_col(step, 0))

    def reduce_columns(chunk):
        arrived(brecv.at[chunk], b2r.at[chunk])
        ball[x, chunk] = (bsum[chunk, y] + brecv[chunk, 0]) + (brecv[chunk, 1] + brecv[chunk, 2])
        for step in (2, 1, 3):
            send(ball.at[x, chunk], ball.at[x, chunk], b3s, b3r, at_x(step))

    def mix_rows(chunk):
        loads_x[chunk].wait()
        tiles = []
        for group in range(8):
            sign = jnp.concatenate(
                [row_sign[2 * group : 2 * group + 1], row_sign[2 * group + 1 : 2 * group + 2]], axis=1
            )
            tiles.append(xbuf[chunk, :, group * 256 : (group + 1) * 256] * sign)
        mixed = jnp.dot(jnp.concatenate(tiles, axis=0), hmat[...], preferred_element_type=F32)
        for tile in range(2):
            parts = butterfly(
                [mixed[g * 32 : (g + 1) * 32, tile * 128 : (tile + 1) * 128] for g in range(8)]
            )
            for g in range(8):
                rmix[g * 2 + tile] = parts[g]
        for k in range(16):
            block = row_blocks[k]
            sign = (1 - 2 * parity((block // 32) & row)).astype(F32) * SCALE
            kept = rmix[(block % 32) // 2]
            above, below = kept[:16], kept[16:]
            straight = jnp.where(low, above, below)
            crossed = pltpu.roll(jnp.where(low, below, above), 64, 1)
            asend[chunk, k] = jnp.where((lane_high ^ (block % 2)) == 0, straight, crossed) * sign
        if chunk == 0:
            pl.semaphore_wait(barrier, len(partners))
        for step in (2, 1, 3):
            first_k = ((x + step) % 4) * 4
            send(asend.at[chunk, pl.ds(first_k, 4)], xrecv.at[chunk, step - 1], xs, xr.at[chunk], at_x(step))

    def reduce_x(chunk):
        arrived(xrecv.at[chunk], xr.at[chunk])
        own = asend[chunk, pl.ds(x * 4, 4)]
        asum[chunk] = (own + xrecv[chunk, 0]) + (xrecv[chunk, 1] + xrecv[chunk, 2])
        for step in (2, 1, 3):
            send(asum.at[chunk, (zh + step) % 4], zrecv.at[chunk, step - 1], zs, zr.at[chunk], at_zh(step))

    def reduce_zh(chunk):
        arrived(zrecv.at[chunk], zr.at[chunk])
        aall[col, chunk] = (asum[chunk, zh] + zrecv[chunk, 0]) + (zrecv[chunk, 1] + zrecv[chunk, 2])
        for dy, dc in around:
            send(aall.at[col, chunk], aall.at[col, chunk], ys, yr.at[chunk], at_col(dy, dc))

    mix_rows(0)
    for load in small[2:]:
        load.wait()
    col_sign = (1 - 2 * col_bits[...]).astype(F32).astype(BF16)
    mix_columns(0)
    for chunk in range(1, CHUNKS):
        mix_rows(chunk)
        mix_columns(chunk)
        pair_columns(chunk - 1)
    pair_columns(CHUNKS - 1)
    reduce_x(0)
    for chunk in range(1, CHUNKS):
        reduce_x(chunk)
        reduce_columns(chunk - 1)
    reduce_columns(CHUNKS - 1)
    for chunk in range(CHUNKS):
        reduce_zh(chunk)

    arrived(ball.at[pl.ds(0, 3)], b3r)

    def product(first, second):
        return lax.dot_general(first, second, (((0,), (0,)), ((), ())), preferred_element_type=F32)

    full = None
    for chunk in range(CHUNKS):
        right_high, right_low = split(jnp.concatenate(
            [ball[:, chunk, :, half * 16 : (half + 1) * 16, :].reshape(128, 128) for half in range(2)],
            axis=1,
        ))
        arrived(aall.at[pl.ds(0, 7), chunk], yr.at[chunk])
        left_high, left_low = split(aall[:, chunk].reshape(128, 128))
        term = (
            product(left_high, right_high)
            + product(left_high, right_low)
            + product(left_low, right_high)
        )
        full = term if full is None else full + term
    psend[...] = full[:64, :128] + full[64:, 128:]
    send(psend, precv, ps, pr, other_seq)
    arrived(precv, pr)
    out[0] = psend[...] + precv[...]
    arrived(asend.at[:, pl.ds(0, 12)], xs)
    arrived(asum.at[:, pl.ds(0, 3)], zs)
    arrived(aall.at[pl.ds(0, 7)], ys)
    arrived(bpair, b1s)
    arrived(brecv, b2s)
    arrived(ball.at[pl.ds(0, 3)], b3s)
    arrived(psend, ps)


def body(out_grads, layer_inputs, row_bits, col_bits, row_blocks, col_blocks):
    vmem = pl.BlockSpec(memory_space=pltpu.VMEM)
    hbm = pl.BlockSpec(memory_space=pl.ANY)
    dma = pltpu.SemaphoreType.DMA
    return pl.pallas_call(
        kernel,
        out_shape=pltpu.VMEM((1, 64, 128), F32),
        in_specs=[hbm] * 6,
        out_specs=vmem,
        scratch_shapes=[
            pltpu.SMEM((16,), jnp.int32),
            pltpu.SMEM((8,), jnp.int32),
            pltpu.VMEM((16, 128), jnp.int32),
            pltpu.VMEM((8, 128), jnp.int32),
            pltpu.VMEM((CHUNKS, 32, 2048), BF16),
            pltpu.VMEM((CHUNKS, 2, 32, 1024), BF16),
            pltpu.VMEM((256, 256), BF16),
            pltpu.VMEM((16, 32, 128), F32),
            pltpu.VMEM((8, 64, 128), F32),
            pltpu.VMEM((CHUNKS, 16, 16, 128), F32),
            pltpu.VMEM((CHUNKS, 3, 4, 16, 128), F32),
            pltpu.VMEM((CHUNKS, 4, 16, 128), F32),
            pltpu.VMEM((CHUNKS, 3, 16, 128), F32),
            pltpu.VMEM((8, CHUNKS, 16, 128), F32),
            pltpu.VMEM((CHUNKS, 2, 4, 2, 32, 128), F32),
            pltpu.VMEM((CHUNKS, 4, 2, 32, 128), F32),
            pltpu.VMEM((CHUNKS, 4, 2, 32, 128), F32),
            pltpu.VMEM((CHUNKS, 3, 2, 32, 128), F32),
            pltpu.VMEM((4, 4, 2, 32, 128), F32),
            pltpu.VMEM((64, 128), F32),
            pltpu.VMEM((64, 128), F32),
            dma((CHUNKS,)), dma((CHUNKS,)), dma((4,)),
            dma(()), dma((CHUNKS,)),
            dma(()), dma((CHUNKS,)),
            dma(()), dma((CHUNKS,)),
            dma(()), dma((CHUNKS,)),
            dma(()), dma((CHUNKS,)),
            dma(()), dma(()),
            dma(()), dma(()),
        ],
        compiler_params=pltpu.CompilerParams(collective_id=0, has_side_effects=True),
        name="sketch",
    )(
        row_blocks, col_blocks, row_bits.reshape(16, 128), col_bits.reshape(8, 128),
        out_grads, layer_inputs,
    )


def solution(mesh):
    in_specs = (P(None, "seq", "row"), P(None, "seq", "col"), P("row"), P("col"), P(), P())
    out_specs = P(None, "row", "col")
    return jax.shard_map(body, mesh=mesh, in_specs=in_specs, out_specs=out_specs, check_vma=False)
```

```python
import math

import jax
import jax.numpy as jnp
from jax import lax
from jax.experimental import pallas as pl
from jax.experimental.pallas import tpu as pltpu
from jax.sharding import PartitionSpec as P

D = 8192
FF = 28672
FFP = 32768
SCALE = 1.0 / math.sqrt(FFP * D)
MESH = pl.DeviceIdType.MESH
CHUNKS = 4
TURNED = 1
F32 = jnp.float32
BF16 = jnp.bfloat16


def parity(value):
    value = value ^ (value >> 4)
    value = value ^ (value >> 2)
    value = value ^ (value >> 1)
    return value & 1


def butterfly(parts):
    stride = 1
    while stride < len(parts):
        for at in range(len(parts)):
            if not at & stride:
                low, high = parts[at], parts[at + stride]
                parts[at], parts[at + stride] = low + high, low - high
        stride *= 2
    return parts


def split(value):
    high = value.astype(BF16)
    return high, (value - high.astype(F32)).astype(BF16)


def kernel(
    row_blocks_in, col_blocks_in, row_bits_in, col_bits_in, grads, inputs, out,
    row_blocks, col_blocks, row_bits, col_bits,
    xbuf, ybuf, hmat, rmix, cmix, asend, xrecv, asum, zrecv, aall,
    zturn, zsum, xturn, bsend, bpair, bsum, brecv, ball, psend, precv,
    load_x, load_y, load_s, xs, xr, zs, zr, ys, yr, zts, ztr, xts, xtr,
    b1s, b1r, b2s, b2r, b3s, b3r, ps, pr,
    in_x, in_zh, in_y,
):
    row, col, seq = lax.axis_index("row"), lax.axis_index("col"), lax.axis_index("seq")
    x, zh = row // 4, row % 4
    y, core = col // 2, col % 2

    def at_x(step):
        return {"row": ((x + step) % 4) * 4 + zh}

    def at_zh(step):
        return {"row": x * 4 + (zh + step) % 4}

    def at_col(dy, dc):
        return {"col": ((y + dy) % 4) * 2 + (core + dc) % 2}

    steps_x = steps_y = steps_zh = (2, 1, 3)
    other_seq = {"seq": 1 - seq}

    small = [
        pltpu.make_async_copy(src, dst, load_s.at[at])
        for at, (src, dst) in enumerate((
            (row_bits_in, row_bits), (row_blocks_in, row_blocks),
            (col_bits_in, col_bits), (col_blocks_in, col_blocks),
        ))
    ]
    loads_x = []
    for chunk in range(CHUNKS):
        start = pl.multiple_of(col * 128 + chunk * 32, 32)
        loads_x.append(
            pltpu.make_async_copy(grads.at[0, pl.ds(start, 32)], xbuf.at[chunk], load_x.at[chunk])
        )
    loads_y = [
        pltpu.make_async_copy(
            inputs.at[0, pl.ds(pl.multiple_of((x * 2 + half) * 128 + chunk * 32, 32), 32)],
            ybuf.at[chunk, half], load_y.at[chunk],
        )
        for chunk in range(CHUNKS)
        for half in range(2)
    ]
    for load in loads_x[:1] + small[:2] + loads_x[1:2] + small[2:] + loads_y[:2] + loads_x[2:] + loads_y[2:]:
        load.start()

    barrier = pltpu.get_barrier_semaphore()
    partners = [at_x(1), at_x(3), at_col(1, 0), at_col(3, 0), at_col(1, 1), at_col(3, 1)]
    partners += [at_zh(1), at_zh(3), at_col(0, 1), other_seq]
    for partner in partners:
        pl.semaphore_signal(barrier, inc=1, device_id=partner, device_id_type=MESH)

    def send(src, dst, send_sem, recv_sem, device):
        pltpu.make_async_remote_copy(
            src_ref=src, dst_ref=dst, send_sem=send_sem, recv_sem=recv_sem,
            device_id=device, device_id_type=MESH,
        ).start()

    def arrived(ref, sem):
        pltpu.make_async_copy(ref, ref, sem).wait()

    first = lax.broadcasted_iota(jnp.int32, (256, 256), 0)
    second = lax.broadcasted_iota(jnp.int32, (256, 256), 1)
    hmat[...] = (1 - 2 * parity(first & second)).astype(F32).astype(BF16)
    lane_high = lax.broadcasted_iota(jnp.int32, (16, 128), 1) // 64
    low = lane_high == 0
    place = lax.broadcasted_iota(jnp.int32, (16, 128), 0) * 128
    place = place + lax.broadcasted_iota(jnp.int32, (16, 128), 1) + row * 2048
    for load in small[:2]:
        load.wait()
    row_slots = [row_blocks[k] % 32 for k in range(16)]
    row_signs = [
        (1 - 2 * parity((row_blocks[k] // 32) & row)).astype(F32) * SCALE for k in range(16)
    ]
    row_sign = jnp.where(place < FF, (1 - 2 * row_bits[...]).astype(F32), 0.0).astype(BF16)

    def mix_columns(chunk):
        arrived(ybuf.at[chunk], load_y.at[chunk])
        tiles = []
        for half in range(2):
            for group in range(4):
                sign = jnp.concatenate(
                    [col_sign[2 * group : 2 * group + 1], col_sign[2 * group + 1 : 2 * group + 2]], axis=1
                )
                tiles.append(ybuf[chunk, half, :, group * 256 : (group + 1) * 256] * sign)
        mixed = jnp.dot(jnp.concatenate(tiles, axis=0), hmat[...], preferred_element_type=F32)
        for half in range(2):
            for tile in range(2):
                parts = butterfly([
                    mixed[(half * 4 + g) * 32 : (half * 4 + g + 1) * 32, tile * 128 : (tile + 1) * 128]
                    for g in range(4)
                ])
                for g in range(4):
                    cmix[g * 2 + tile, half * 32 : (half + 1) * 32] = parts[g]
        for m in range(8):
            kept = cmix[col_slots[m]] * col_signs[m]
            bsend[chunk, m % 2, m // 2] = kept.reshape(2, 32, 128)
        send(bsend.at[chunk, 1 - core], bpair.at[chunk], b1s, b1r.at[chunk], at_col(0, 1))

    def pair_columns(chunk):
        arrived(bpair.at[chunk], b1r.at[chunk])
        bsum[chunk] = bsend[chunk, core] + bpair[chunk]
        for step in steps_y:
            send(bsum.at[chunk, (y + step) % 4], brecv.at[chunk, step - 1], b2s, b2r.at[chunk], at_col(step, 0))

    def reduce_columns(chunk):
        arrived(brecv.at[chunk], b2r.at[chunk])
        ball[x, chunk] = (bsum[chunk, y] + brecv[chunk, 0]) + (brecv[chunk, 1] + brecv[chunk, 2])
        for step in steps_x:
            send(ball.at[x, chunk], ball.at[x, chunk], b3s, b3r.at[chunk], at_x(step))

    def mix_rows(chunk):
        loads_x[chunk].wait()
        tiles = []
        for group in range(8):
            sign = jnp.concatenate(
                [row_sign[2 * group : 2 * group + 1], row_sign[2 * group + 1 : 2 * group + 2]], axis=1
            )
            tiles.append(xbuf[chunk, :, group * 256 : (group + 1) * 256] * sign)
        mixed = jnp.dot(jnp.concatenate(tiles, axis=0), hmat[...], preferred_element_type=F32)
        for tile in range(2):
            parts = butterfly(
                [mixed[g * 32 : (g + 1) * 32, tile * 128 : (tile + 1) * 128] for g in range(8)]
            )
            for g in range(8):
                rmix[g * 2 + tile] = parts[g]
        for k in range(16):
            kept = rmix[row_slots[k] // 2]
            above, below = kept[:16], kept[16:]
            straight = jnp.where(low, above, below)
            crossed = pltpu.roll(jnp.where(low, below, above), 64, 1)
            slot = k if chunk != TURNED else (k % 4) * 4 + k // 4
            asend[chunk, slot] = jnp.where((lane_high ^ (row_slots[k] % 2)) == 0, straight, crossed) * row_signs[k]

    def send_rows(chunk, steps=(2, 1, 3)):
        for step in steps:
            if chunk == TURNED:
                first_k = ((zh + step) % 4) * 4
                send(asend.at[chunk, pl.ds(first_k, 4)], zturn.at[step - 1], zts, ztr, at_zh(step))
            else:
                first_k = ((x + step) % 4) * 4
                send(asend.at[chunk, pl.ds(first_k, 4)], xrecv.at[chunk, step - 1], xs, xr.at[chunk], at_x(step))

    def reduce_x(chunk):
        arrived(xrecv.at[chunk], xr.at[chunk])
        own = asend[chunk, pl.ds(x * 4, 4)]
        asum[chunk] = (own + xrecv[chunk, 0]) + (xrecv[chunk, 1] + xrecv[chunk, 2])
        for step in steps_zh:
            send(asum.at[chunk, (zh + step) % 4], zrecv.at[chunk, step - 1], zs, zr.at[chunk], at_zh(step))

    def spread(chunk):
        for step in steps_y:
            for flip in range(2):
                send(aall.at[col, chunk], aall.at[col, chunk], ys, yr.at[chunk], at_col(step, flip))
        send(aall.at[col, chunk], aall.at[col, chunk], ys, yr.at[chunk], at_col(0, 1))

    def reduce_zh(chunk):
        arrived(zrecv.at[chunk], zr.at[chunk])
        aall[col, chunk] = (asum[chunk, zh] + zrecv[chunk, 0]) + (zrecv[chunk, 1] + zrecv[chunk, 2])
        spread(chunk)

    def turned_zh():
        arrived(zturn, ztr)
        own = asend[TURNED, pl.ds(zh * 4, 4)]
        zsum[...] = (own + zturn[0]) + (zturn[1] + zturn[2])
        for step in steps_x:
            send(zsum.at[(x + step) % 4], xturn.at[step - 1], xts, xtr, at_x(step))

    def turned_x():
        arrived(xturn, xtr)
        aall[col, TURNED] = (zsum[x] + xturn[0]) + (xturn[1] + xturn[2])
        spread(TURNED)

    mix_rows(0)
    pl.semaphore_wait(barrier, len(partners))
    pl.semaphore_signal(in_x, inc=1, device_id=at_x(3), device_id_type=MESH)
    pl.semaphore_signal(in_zh, inc=1, device_id=at_zh(3), device_id_type=MESH)
    pl.semaphore_signal(in_y, inc=1, device_id=at_col(3, 0), device_id_type=MESH)
    send_rows(0, (1, 3))
    for load in small[2:]:
        load.wait()
    col_sign = (1 - 2 * col_bits[...]).astype(F32).astype(BF16)
    col_slots = [col_blocks[m] % 8 for m in range(8)]
    col_signs = [(1 - 2 * parity((col_blocks[m] // 8) & col)).astype(F32) for m in range(8)]
    mix_columns(0)
    mix_rows(TURNED)
    send_rows(TURNED, (1, 3))
    pl.semaphore_wait(in_x, 1)
    send_rows(0, (2,))
    pl.semaphore_wait(in_zh, 1)
    send_rows(TURNED, (2,))
    mix_rows(2)
    send_rows(2, steps_x)
    pl.semaphore_wait(in_y, 1)
    pair_columns(0)
    mix_columns(1)
    mix_rows(3)
    send_rows(3, steps_x)
    mix_columns(2)
    pair_columns(1)
    mix_columns(3)
    pair_columns(2)
    pair_columns(3)
    reduce_x(0)
    reduce_x(2)
    reduce_columns(0)
    reduce_x(3)
    turned_zh()
    reduce_columns(1)
    reduce_zh(0)
    reduce_columns(2)
    reduce_zh(2)
    reduce_columns(3)
    turned_x()
    reduce_zh(3)

    def product(first, second):
        return jnp.dot(first, second, preferred_element_type=F32)

    full = None
    for chunk in (0, 2, 1, 3):
        arrived(ball.at[pl.ds(0, 3), chunk], b3r.at[chunk])
        right_high, right_low = split(jnp.concatenate(
            [ball[:, chunk, :, half * 16 : (half + 1) * 16].reshape(128, 128) for half in range(2)],
            axis=0,
        ))
        arrived(aall.at[pl.ds(0, 7), chunk], yr.at[chunk])
        left = aall[:, chunk].reshape(128, 128).T
        left_high, left_low = split(jnp.concatenate([left[:64], left[64:]], axis=1))
        term = (
            product(left_high, right_high)
            + product(left_high, right_low)
            + product(left_low, right_high)
        )
        full = term if full is None else full + term
    psend[...] = full
    send(psend, precv, ps, pr, other_seq)
    arrived(precv, pr)
    out[0] = psend[...] + precv[...]
    arrived(asend.at[pl.ds(0, 3), pl.ds(0, 12)], xs)
    arrived(asum.at[pl.ds(0, 3), pl.ds(0, 3)], zs)
    arrived(zturn, zts)
    arrived(xturn, xts)
    arrived(aall.at[pl.ds(0, 7)], ys)
    arrived(bpair, b1s)
    arrived(brecv, b2s)
    arrived(ball.at[pl.ds(0, 3)], b3s)
    arrived(psend, ps)


def body(out_grads, layer_inputs, row_bits, col_bits, row_blocks, col_blocks):
    vmem = pl.BlockSpec(memory_space=pltpu.VMEM)
    hbm = pl.BlockSpec(memory_space=pl.ANY)
    dma = pltpu.SemaphoreType.DMA
    return pl.pallas_call(
        kernel,
        out_shape=pltpu.VMEM((1, 64, 128), F32),
        in_specs=[hbm] * 6,
        out_specs=vmem,
        scratch_shapes=[
            pltpu.SMEM((16,), jnp.int32),
            pltpu.SMEM((8,), jnp.int32),
            pltpu.VMEM((16, 128), jnp.int32),
            pltpu.VMEM((8, 128), jnp.int32),
            pltpu.VMEM((CHUNKS, 32, 2048), BF16),
            pltpu.VMEM((CHUNKS, 2, 32, 1024), BF16),
            pltpu.VMEM((256, 256), BF16),
            pltpu.VMEM((16, 32, 128), F32),
            pltpu.VMEM((8, 64, 128), F32),
            pltpu.VMEM((CHUNKS, 16, 16, 128), F32),
            pltpu.VMEM((CHUNKS, 3, 4, 16, 128), F32),
            pltpu.VMEM((CHUNKS, 4, 16, 128), F32),
            pltpu.VMEM((CHUNKS, 3, 16, 128), F32),
            pltpu.VMEM((8, CHUNKS, 16, 128), F32),
            pltpu.VMEM((3, 4, 16, 128), F32),
            pltpu.VMEM((4, 16, 128), F32),
            pltpu.VMEM((3, 16, 128), F32),
            pltpu.VMEM((CHUNKS, 2, 4, 2, 32, 128), F32),
            pltpu.VMEM((CHUNKS, 4, 2, 32, 128), F32),
            pltpu.VMEM((CHUNKS, 4, 2, 32, 128), F32),
            pltpu.VMEM((CHUNKS, 3, 2, 32, 128), F32),
            pltpu.VMEM((4, 4, 2, 32, 128), F32),
            pltpu.VMEM((64, 128), F32),
            pltpu.VMEM((64, 128), F32),
            dma((CHUNKS,)), dma((CHUNKS,)), dma((4,)),
            dma(()), dma((CHUNKS,)),
            dma(()), dma((CHUNKS,)),
            dma(()), dma((CHUNKS,)),
            dma(()), dma(()), dma(()), dma(()),
            dma(()), dma((CHUNKS,)),
            dma(()), dma((CHUNKS,)),
            dma(()), dma((CHUNKS,)),
            dma(()), dma(()),
            pltpu.SemaphoreType.REGULAR, pltpu.SemaphoreType.REGULAR, pltpu.SemaphoreType.REGULAR,
        ],
        compiler_params=pltpu.CompilerParams(collective_id=0, has_side_effects=True),
        name="sketch",
    )(
        row_blocks, col_blocks, row_bits.reshape(16, 128), col_bits.reshape(8, 128),
        out_grads, layer_inputs,
    )


def solution(mesh):
    in_specs = (P(None, "seq", "row"), P(None, "seq", "col"), P("row"), P("col"), P(), P())
    out_specs = P(None, "row", "col")
    return jax.shard_map(body, mesh=mesh, in_specs=in_specs, out_specs=out_specs, check_vma=False)
```

```python
import math

import jax
import jax.numpy as jnp
from jax import lax
from jax.experimental import pallas as pl
from jax.experimental.pallas import tpu as pltpu
from jax.sharding import PartitionSpec as P

D = 8192
FF = 28672
FFP = 32768
SCALE = 1.0 / math.sqrt(FFP * D)
MESH = pl.DeviceIdType.MESH
CHUNKS = 4
TURNED = 1
F32 = jnp.float32
BF16 = jnp.bfloat16


def parity(value):
    value = value ^ (value >> 4)
    value = value ^ (value >> 2)
    value = value ^ (value >> 1)
    return value & 1


def butterfly(parts):
    stride = 1
    while stride < len(parts):
        for at in range(len(parts)):
            if not at & stride:
                low, high = parts[at], parts[at + stride]
                parts[at], parts[at + stride] = low + high, low - high
        stride *= 2
    return parts


def split(value):
    high = value.astype(BF16)
    return high, (value - high.astype(F32)).astype(BF16)


def kernel(
    row_blocks_in, col_blocks_in, row_bits_in, col_bits_in, grads, inputs, out,
    row_blocks, col_blocks, row_bits, col_bits,
    xbuf, ybuf, hmat, rmix, cmix, asend, xrecv, asum, zrecv, aall,
    zturn, zsum, xturn, bsend, bpair, bsum, brecv, ball, psend, precv,
    load_x, load_y, load_s, xs, xr, zs, zr, ys, yr, zts, ztr, xts, xtr,
    b1s, b1r, b2s, b2r, b3s, b3r, ps, pr,
    in_zh,
):
    row, col, seq = lax.axis_index("row"), lax.axis_index("col"), lax.axis_index("seq")
    x, zh = row // 4, row % 4
    y, core = col // 2, col % 2

    def at_x(step):
        return {"row": ((x + step) % 4) * 4 + zh}

    def at_zh(step):
        return {"row": x * 4 + (zh + step) % 4}

    def at_col(dy, dc):
        return {"col": ((y + dy) % 4) * 2 + (core + dc) % 2}

    other_seq = {"seq": 1 - seq}

    small = [
        pltpu.make_async_copy(src, dst, load_s.at[at])
        for at, (src, dst) in enumerate((
            (row_bits_in, row_bits), (row_blocks_in, row_blocks),
            (col_bits_in, col_bits), (col_blocks_in, col_blocks),
        ))
    ]
    loads_x = []
    for chunk in range(CHUNKS):
        start = pl.multiple_of(col * 128 + chunk * 32, 32)
        loads_x.append(
            pltpu.make_async_copy(grads.at[0, pl.ds(start, 32)], xbuf.at[chunk], load_x.at[chunk])
        )
    loads_y = [
        pltpu.make_async_copy(
            inputs.at[0, pl.ds(pl.multiple_of((x * 2 + half) * 128 + chunk * 32, 32), 32)],
            ybuf.at[chunk, half], load_y.at[chunk],
        )
        for chunk in range(CHUNKS)
        for half in range(2)
    ]
    for load in loads_x[:1] + small[:2] + loads_x[1:2] + small[2:] + loads_y[:2] + loads_x[2:] + loads_y[2:]:
        load.start()

    barrier = pltpu.get_barrier_semaphore()
    partners = [at_x(step) for step in (2, 1, 3)]
    partners += [at_col(step, flip) for step in (2, 1, 3) for flip in range(2)]
    partners += [at_zh(1), at_zh(3), at_col(0, 1), other_seq]
    for partner in partners:
        pl.semaphore_signal(barrier, inc=1, device_id=partner, device_id_type=MESH)

    def send(src, dst, send_sem, recv_sem, device):
        pltpu.make_async_remote_copy(
            src_ref=src, dst_ref=dst, send_sem=send_sem, recv_sem=recv_sem,
            device_id=device, device_id_type=MESH,
        ).start()

    def arrived(ref, sem):
        pltpu.make_async_copy(ref, ref, sem).wait()

    first = lax.broadcasted_iota(jnp.int32, (256, 256), 0)
    second = lax.broadcasted_iota(jnp.int32, (256, 256), 1)
    hmat[...] = (1 - 2 * parity(first & second)).astype(F32).astype(BF16)
    lane_high = lax.broadcasted_iota(jnp.int32, (16, 128), 1) // 64
    low = lane_high == 0
    place = lax.broadcasted_iota(jnp.int32, (16, 128), 0) * 128
    place = place + lax.broadcasted_iota(jnp.int32, (16, 128), 1) + row * 2048
    for load in small[:2]:
        load.wait()
    row_slots = [row_blocks[k] % 32 for k in range(16)]
    row_signs = [
        (1 - 2 * parity((row_blocks[k] // 32) & row)).astype(F32) * SCALE for k in range(16)
    ]
    row_sign = jnp.where(place < FF, (1 - 2 * row_bits[...]).astype(F32), 0.0).astype(BF16)

    def mix_columns(chunk):
        arrived(ybuf.at[chunk], load_y.at[chunk])
        tiles = []
        for half in range(2):
            for group in range(4):
                sign = jnp.concatenate(
                    [col_sign[2 * group : 2 * group + 1], col_sign[2 * group + 1 : 2 * group + 2]], axis=1
                )
                tiles.append(ybuf[chunk, half, :, group * 256 : (group + 1) * 256] * sign)
        mixed = jnp.dot(jnp.concatenate(tiles, axis=0), hmat[...], preferred_element_type=F32)
        for half in range(2):
            for tile in range(2):
                parts = butterfly([
                    mixed[(half * 4 + g) * 32 : (half * 4 + g + 1) * 32, tile * 128 : (tile + 1) * 128]
                    for g in range(4)
                ])
                for g in range(4):
                    cmix[g * 2 + tile, half * 32 : (half + 1) * 32] = parts[g]
        for m in range(8):
            kept = cmix[col_slots[m]] * col_signs[m]
            bsend[chunk, m % 2, m // 2] = kept.reshape(2, 32, 128)
        send(bsend.at[chunk, 1 - core], bpair.at[chunk], b1s, b1r.at[chunk], at_col(0, 1))

    def pair_columns(chunk):
        arrived(bpair.at[chunk], b1r.at[chunk])
        bsum[chunk] = bsend[chunk, core] + bpair[chunk]
        for step in (2, 1, 3):
            send(bsum.at[chunk, (y + step) % 4], brecv.at[chunk, step - 1], b2s, b2r.at[chunk], at_col(step, 0))

    def reduce_columns(chunk):
        arrived(brecv.at[chunk], b2r.at[chunk])
        ball[x, chunk] = (bsum[chunk, y] + brecv[chunk, 0]) + (brecv[chunk, 1] + brecv[chunk, 2])
        for step in (2, 1, 3):
            send(ball.at[x, chunk], ball.at[x, chunk], b3s, b3r.at[chunk], at_x(step))

    def mix_rows(chunk):
        loads_x[chunk].wait()
        tiles = []
        for group in range(8):
            sign = jnp.concatenate(
                [row_sign[2 * group : 2 * group + 1], row_sign[2 * group + 1 : 2 * group + 2]], axis=1
            )
            tiles.append(xbuf[chunk, :, group * 256 : (group + 1) * 256] * sign)
        mixed = jnp.dot(jnp.concatenate(tiles, axis=0), hmat[...], preferred_element_type=F32)
        for tile in range(2):
            parts = butterfly(
                [mixed[g * 32 : (g + 1) * 32, tile * 128 : (tile + 1) * 128] for g in range(8)]
            )
            for g in range(8):
                rmix[g * 2 + tile] = parts[g]
        for k in range(16):
            kept = rmix[row_slots[k] // 2]
            above, below = kept[:16], kept[16:]
            straight = jnp.where(low, above, below)
            crossed = pltpu.roll(jnp.where(low, below, above), 64, 1)
            slot = k if chunk != TURNED else (k % 4) * 4 + k // 4
            asend[chunk, slot] = jnp.where((lane_high ^ (row_slots[k] % 2)) == 0, straight, crossed) * row_signs[k]

    def send_rows(chunk, steps=(2, 1, 3)):
        for step in steps:
            if chunk == TURNED:
                first_k = ((zh + step) % 4) * 4
                send(asend.at[chunk, pl.ds(first_k, 4)], zturn.at[step - 1], zts, ztr, at_zh(step))
            else:
                first_k = ((x + step) % 4) * 4
                send(asend.at[chunk, pl.ds(first_k, 4)], xrecv.at[chunk, step - 1], xs, xr.at[chunk], at_x(step))

    def reduce_x(chunk):
        arrived(xrecv.at[chunk], xr.at[chunk])
        own = asend[chunk, pl.ds(x * 4, 4)]
        asum[chunk] = (own + xrecv[chunk, 0]) + (xrecv[chunk, 1] + xrecv[chunk, 2])
        for step in (2, 1, 3):
            send(asum.at[chunk, (zh + step) % 4], zrecv.at[chunk, step - 1], zs, zr.at[chunk], at_zh(step))

    def spread(chunk):
        for step in (2, 1, 3):
            for flip in range(2):
                send(aall.at[col, chunk], aall.at[col, chunk], ys, yr.at[chunk], at_col(step, flip))
        send(aall.at[col, chunk], aall.at[col, chunk], ys, yr.at[chunk], at_col(0, 1))

    def reduce_zh(chunk):
        arrived(zrecv.at[chunk], zr.at[chunk])
        aall[col, chunk] = (asum[chunk, zh] + zrecv[chunk, 0]) + (zrecv[chunk, 1] + zrecv[chunk, 2])
        spread(chunk)

    def turned_zh():
        arrived(zturn, ztr)
        own = asend[TURNED, pl.ds(zh * 4, 4)]
        zsum[...] = (own + zturn[0]) + (zturn[1] + zturn[2])
        for step in (2, 1, 3):
            send(zsum.at[(x + step) % 4], xturn.at[step - 1], xts, xtr, at_x(step))

    def turned_x():
        arrived(xturn, xtr)
        aall[col, TURNED] = (zsum[x] + xturn[0]) + (xturn[1] + xturn[2])
        spread(TURNED)

    mix_rows(0)
    pl.semaphore_wait(barrier, len(partners))
    pl.semaphore_signal(in_zh, inc=1, device_id=at_zh(3), device_id_type=MESH)
    send_rows(0)
    for load in small[2:]:
        load.wait()
    col_sign = (1 - 2 * col_bits[...]).astype(F32).astype(BF16)
    col_slots = [col_blocks[m] % 8 for m in range(8)]
    col_signs = [(1 - 2 * parity((col_blocks[m] // 8) & col)).astype(F32) for m in range(8)]
    mix_columns(0)
    mix_rows(TURNED)
    send_rows(TURNED, (1, 3))
    mix_rows(2)
    send_rows(2)
    pl.semaphore_wait(in_zh, 1)
    send_rows(TURNED, (2,))
    pair_columns(0)
    mix_columns(1)
    mix_rows(3)
    send_rows(3)
    mix_columns(2)
    pair_columns(1)
    mix_columns(3)
    pair_columns(2)
    pair_columns(3)
    reduce_x(0)
    reduce_x(2)
    reduce_columns(0)
    reduce_x(3)
    turned_zh()
    reduce_columns(1)
    reduce_zh(0)
    reduce_columns(2)
    reduce_zh(2)
    reduce_columns(3)
    turned_x()
    reduce_zh(3)

    def product(first, second):
        return jnp.dot(first, second, preferred_element_type=F32)

    full = None
    for chunk in (0, 2, 1, 3):
        arrived(ball.at[pl.ds(0, 3), chunk], b3r.at[chunk])
        right_high, right_low = split(jnp.concatenate(
            [ball[:, chunk, :, half * 16 : (half + 1) * 16].reshape(128, 128) for half in range(2)],
            axis=0,
        ))
        arrived(aall.at[pl.ds(0, 7), chunk], yr.at[chunk])
        left = aall[:, chunk].reshape(128, 128).T
        left_high, left_low = split(jnp.concatenate([left[:64], left[64:]], axis=1))
        term = (
            product(left_high, right_high)
            + product(left_high, right_low)
            + product(left_low, right_high)
        )
        full = term if full is None else full + term
    psend[...] = full
    send(psend, precv, ps, pr, other_seq)
    arrived(precv, pr)
    out[0] = psend[...] + precv[...]
    arrived(asend.at[pl.ds(0, 3), pl.ds(0, 12)], xs)
    arrived(asum.at[pl.ds(0, 3), pl.ds(0, 3)], zs)
    arrived(zturn, zts)
    arrived(xturn, xts)
    arrived(aall.at[pl.ds(0, 7)], ys)
    arrived(bpair, b1s)
    arrived(brecv, b2s)
    arrived(ball.at[pl.ds(0, 3)], b3s)
    arrived(psend, ps)


def body(out_grads, layer_inputs, row_bits, col_bits, row_blocks, col_blocks):
    vmem = pl.BlockSpec(memory_space=pltpu.VMEM)
    hbm = pl.BlockSpec(memory_space=pl.ANY)
    dma = pltpu.SemaphoreType.DMA
    return pl.pallas_call(
        kernel,
        out_shape=pltpu.VMEM((1, 64, 128), F32),
        in_specs=[hbm] * 6,
        out_specs=vmem,
        scratch_shapes=[
            pltpu.SMEM((16,), jnp.int32),
            pltpu.SMEM((8,), jnp.int32),
            pltpu.VMEM((16, 128), jnp.int32),
            pltpu.VMEM((8, 128), jnp.int32),
            pltpu.VMEM((CHUNKS, 32, 2048), BF16),
            pltpu.VMEM((CHUNKS, 2, 32, 1024), BF16),
            pltpu.VMEM((256, 256), BF16),
            pltpu.VMEM((16, 32, 128), F32),
            pltpu.VMEM((8, 64, 128), F32),
            pltpu.VMEM((CHUNKS, 16, 16, 128), F32),
            pltpu.VMEM((CHUNKS, 3, 4, 16, 128), F32),
            pltpu.VMEM((CHUNKS, 4, 16, 128), F32),
            pltpu.VMEM((CHUNKS, 3, 16, 128), F32),
            pltpu.VMEM((8, CHUNKS, 16, 128), F32),
            pltpu.VMEM((3, 4, 16, 128), F32),
            pltpu.VMEM((4, 16, 128), F32),
            pltpu.VMEM((3, 16, 128), F32),
            pltpu.VMEM((CHUNKS, 2, 4, 2, 32, 128), F32),
            pltpu.VMEM((CHUNKS, 4, 2, 32, 128), F32),
            pltpu.VMEM((CHUNKS, 4, 2, 32, 128), F32),
            pltpu.VMEM((CHUNKS, 3, 2, 32, 128), F32),
            pltpu.VMEM((4, 4, 2, 32, 128), F32),
            pltpu.VMEM((64, 128), F32),
            pltpu.VMEM((64, 128), F32),
            dma((CHUNKS,)), dma((CHUNKS,)), dma((4,)),
            dma(()), dma((CHUNKS,)),
            dma(()), dma((CHUNKS,)),
            dma(()), dma((CHUNKS,)),
            dma(()), dma(()), dma(()), dma(()),
            dma(()), dma((CHUNKS,)),
            dma(()), dma((CHUNKS,)),
            dma(()), dma((CHUNKS,)),
            dma(()), dma(()),
            pltpu.SemaphoreType.REGULAR,
        ],
        compiler_params=pltpu.CompilerParams(collective_id=0, has_side_effects=True),
        name="sketch",
    )(
        row_blocks, col_blocks, row_bits.reshape(16, 128), col_bits.reshape(8, 128),
        out_grads, layer_inputs,
    )


def solution(mesh):
    in_specs = (P(None, "seq", "row"), P(None, "seq", "col"), P("row"), P("col"), P(), P())
    out_specs = P(None, "row", "col")
    return jax.shard_map(body, mesh=mesh, in_specs=in_specs, out_specs=out_specs, check_vma=False)
```

```python
import math

import jax
import jax.numpy as jnp
from jax import lax
from jax.experimental import pallas as pl
from jax.experimental.pallas import tpu as pltpu
from jax.sharding import PartitionSpec as P

D = 8192
FF = 28672
FFP = 32768
SCALE = 1.0 / math.sqrt(FFP * D)
MESH = pl.DeviceIdType.MESH
CHUNKS = 4
TURNED = 1
LAST = 3
ROW_TILE, COL_TILE = 16 * 128 * 4, 64 * 128 * 4
SENT = (
    3 * 3 * 4 * ROW_TILE + 3 * 4 * ROW_TILE + 3 * 3 * ROW_TILE + 3 * ROW_TILE + CHUNKS * 7 * ROW_TILE
    + CHUNKS * 4 * COL_TILE + CHUNKS * 3 * COL_TILE + CHUNKS * 3 * COL_TILE + COL_TILE
)
F32 = jnp.float32
BF16 = jnp.bfloat16


def parity(value):
    value = value ^ (value >> 4)
    value = value ^ (value >> 2)
    value = value ^ (value >> 1)
    return value & 1


def butterfly(parts):
    stride = 1
    while stride < len(parts):
        for at in range(len(parts)):
            if not at & stride:
                low, high = parts[at], parts[at + stride]
                parts[at], parts[at + stride] = low + high, low - high
        stride *= 2
    return parts


def split(value):
    high = value.astype(BF16)
    return high, (value - high.astype(F32)).astype(BF16)


def kernel(
    row_blocks_in, col_blocks_in, row_bits_in, col_bits_in, grads, inputs, out,
    row_blocks, col_blocks, row_bits, col_bits,
    xbuf, ybuf, hmat, rmix, cmix, asend, xrecv, asum, zrecv, aall,
    zturn, zsum, xturn, bsend, bpair, bsum, brecv, ball, psend, precv,
    load_x, load_y, load_s, sent, xr, zr, yr, b1r, b2r, b3r, pr, in_zh, sizes,
):
    row, col, seq = lax.axis_index("row"), lax.axis_index("col"), lax.axis_index("seq")
    x, zh = row // 4, row % 4
    y, core = col // 2, col % 2

    def at_x(step):
        return {"row": ((x + step) % 4) * 4 + zh}

    def at_zh(step):
        return {"row": x * 4 + (zh + step) % 4}

    def at_col(dy, dc):
        return {"col": ((y + dy) % 4) * 2 + (core + dc) % 2}

    other_seq = {"seq": 1 - seq}

    small = [
        pltpu.make_async_copy(src, dst, load_s.at[at])
        for at, (src, dst) in enumerate((
            (row_bits_in, row_bits), (row_blocks_in, row_blocks),
            (col_bits_in, col_bits), (col_blocks_in, col_blocks),
        ))
    ]
    loads_x = []
    for chunk in range(CHUNKS):
        start = pl.multiple_of(col * 128 + chunk * 32, 32)
        loads_x.append(
            pltpu.make_async_copy(grads.at[0, pl.ds(start, 32)], xbuf.at[chunk], load_x.at[min(chunk, 1)])
        )
    loads_y = [
        pltpu.make_async_copy(
            inputs.at[0, pl.ds(pl.multiple_of((x * 2 + half) * 128 + chunk * 32, 32), 32)],
            ybuf.at[chunk, half], load_y,
        )
        for chunk in range(CHUNKS)
        for half in range(2)
    ]
    for load in loads_x[:1] + small[:2] + loads_x[1:2] + small[2:] + loads_y[:2] + loads_x[2:] + loads_y[2:]:
        load.start()

    barrier = pltpu.get_barrier_semaphore()
    partners = [at_x(step) for step in (2, 1, 3)]
    partners += [at_col(step, flip) for step in (2, 1, 3) for flip in range(2)]
    partners += [at_zh(1), at_zh(3), at_col(0, 1), other_seq]
    for partner in partners:
        pl.semaphore_signal(barrier, inc=1, device_id=partner, device_id_type=MESH)

    def send(src, dst, recv_sem, device):
        pltpu.make_async_remote_copy(
            src_ref=src, dst_ref=dst, send_sem=sent, recv_sem=recv_sem,
            device_id=device, device_id_type=MESH,
        ).start()

    def arrived(ref, sem):
        pltpu.make_async_copy(ref, ref, sem).wait()

    first = lax.broadcasted_iota(jnp.int32, (256, 256), 0)
    second = lax.broadcasted_iota(jnp.int32, (256, 256), 1)
    hmat[...] = (1 - 2 * parity(first & second)).astype(F32).astype(BF16)
    lane_high = lax.broadcasted_iota(jnp.int32, (16, 128), 1) // 64
    low = lane_high == 0
    place = lax.broadcasted_iota(jnp.int32, (16, 128), 0) * 128
    place = place + lax.broadcasted_iota(jnp.int32, (16, 128), 1) + row * 2048
    for load in small[:2]:
        load.wait()
    row_slots = [row_blocks[k] % 32 for k in range(16)]
    row_signs = [
        (1 - 2 * parity((row_blocks[k] // 32) & row)).astype(F32) * SCALE for k in range(16)
    ]
    row_sign = jnp.where(place < FF, (1 - 2 * row_bits[...]).astype(F32), 0.0).astype(BF16)

    def mix_columns(chunk):
        if chunk == 0:
            arrived(ybuf, load_y)
        tiles = []
        for half in range(2):
            for group in range(4):
                sign = jnp.concatenate(
                    [col_sign[2 * group : 2 * group + 1], col_sign[2 * group + 1 : 2 * group + 2]], axis=1
                )
                tiles.append(ybuf[chunk, half, :, group * 256 : (group + 1) * 256] * sign)
        mixed = jnp.dot(jnp.concatenate(tiles, axis=0), hmat[...], preferred_element_type=F32)
        for half in range(2):
            for tile in range(2):
                parts = butterfly([
                    mixed[(half * 4 + g) * 32 : (half * 4 + g + 1) * 32, tile * 128 : (tile + 1) * 128]
                    for g in range(4)
                ])
                for g in range(4):
                    cmix[g * 2 + tile, half * 32 : (half + 1) * 32] = parts[g]
        for m in range(8):
            kept = cmix[col_slots[m]] * col_signs[m]
            bsend[chunk, m % 2, m // 2] = kept.reshape(2, 32, 128)
        send(bsend.at[chunk, 1 - core], bpair.at[chunk], b1r.at[chunk], at_col(0, 1))

    def pair_columns(chunk):
        arrived(bpair.at[chunk], b1r.at[chunk])
        bsum[chunk] = bsend[chunk, core] + bpair[chunk]
        for step in (2, 1, 3):
            send(bsum.at[chunk, (y + step) % 4], brecv.at[chunk, step - 1], b2r.at[chunk], at_col(step, 0))

    def reduce_columns(chunk):
        arrived(brecv.at[chunk], b2r.at[chunk])
        ball[x, chunk] = (bsum[chunk, y] + brecv[chunk, 0]) + (brecv[chunk, 1] + brecv[chunk, 2])
        for step in (2, 1, 3):
            send(ball.at[x, chunk], ball.at[x, chunk], b3r.at[chunk], at_x(step))

    def mix_rows(chunk):
        if chunk == 0:
            arrived(xbuf.at[0], load_x.at[0])
        if chunk == 1:
            arrived(xbuf.at[pl.ds(1, CHUNKS - 1)], load_x.at[1])
        tiles = []
        for group in range(8):
            sign = jnp.concatenate(
                [row_sign[2 * group : 2 * group + 1], row_sign[2 * group + 1 : 2 * group + 2]], axis=1
            )
            tiles.append(xbuf[chunk, :, group * 256 : (group + 1) * 256] * sign)
        mixed = jnp.dot(jnp.concatenate(tiles, axis=0), hmat[...], preferred_element_type=F32)
        for tile in range(2):
            parts = butterfly(
                [mixed[g * 32 : (g + 1) * 32, tile * 128 : (tile + 1) * 128] for g in range(8)]
            )
            for g in range(8):
                rmix[g * 2 + tile] = parts[g]
        for k in range(16):
            kept = rmix[row_slots[k] // 2]
            above, below = kept[:16], kept[16:]
            straight = jnp.where(low, above, below)
            crossed = pltpu.roll(jnp.where(low, below, above), 64, 1)
            slot = k if chunk != TURNED else (k % 4) * 4 + k // 4
            asend[chunk, slot] = jnp.where((lane_high ^ (row_slots[k] % 2)) == 0, straight, crossed) * row_signs[k]

    def send_rows(chunk, steps=(2, 1, 3)):
        for step in steps:
            if chunk == TURNED:
                first_k = ((zh + step) % 4) * 4
                send(asend.at[chunk, pl.ds(first_k, 4)], zturn.at[step - 1], zr.at[TURNED], at_zh(step))
            else:
                first_k = ((x + step) % 4) * 4
                send(asend.at[chunk, pl.ds(first_k, 4)], xrecv.at[chunk, step - 1], xr.at[chunk], at_x(step))

    def reduce_x(chunk):
        arrived(xrecv.at[chunk], xr.at[chunk])
        own = asend[chunk, pl.ds(x * 4, 4)]
        asum[chunk] = (own + xrecv[chunk, 0]) + (xrecv[chunk, 1] + xrecv[chunk, 2])
        for step in (2, 1, 3):
            send(asum.at[chunk, (zh + step) % 4], zrecv.at[chunk, step - 1], zr.at[chunk], at_zh(step))

    def spread(chunk):
        for step in (2, 1, 3):
            for flip in range(2):
                send(aall.at[col, chunk], aall.at[col, chunk], yr.at[chunk], at_col(step, flip))
        send(aall.at[col, chunk], aall.at[col, chunk], yr.at[chunk], at_col(0, 1))

    def reduce_zh(chunk):
        arrived(zrecv.at[chunk], zr.at[chunk])
        aall[col, chunk] = (asum[chunk, zh] + zrecv[chunk, 0]) + (zrecv[chunk, 1] + zrecv[chunk, 2])
        spread(chunk)

    def turned_zh():
        arrived(zturn, zr.at[TURNED])
        own = asend[TURNED, pl.ds(zh * 4, 4)]
        zsum[...] = (own + zturn[0]) + (zturn[1] + zturn[2])
        for step in (2, 1, 3):
            send(zsum.at[(x + step) % 4], xturn.at[step - 1], xr.at[TURNED], at_x(step))

    def turned_x():
        arrived(xturn, xr.at[TURNED])
        aall[col, TURNED] = (zsum[x] + xturn[0]) + (xturn[1] + xturn[2])
        spread(TURNED)

    mix_rows(0)
    pl.semaphore_wait(barrier, len(partners))
    pl.semaphore_signal(in_zh, inc=1, device_id=at_zh(3), device_id_type=MESH)
    send_rows(0)
    for load in small[2:]:
        load.wait()
    col_sign = (1 - 2 * col_bits[...]).astype(F32).astype(BF16)
    col_slots = [col_blocks[m] % 8 for m in range(8)]
    col_signs = [(1 - 2 * parity((col_blocks[m] // 8) & col)).astype(F32) for m in range(8)]
    mix_columns(0)
    mix_rows(TURNED)
    send_rows(TURNED, (1, 3))
    mix_rows(2)
    send_rows(2)
    pl.semaphore_wait(in_zh, 1)
    send_rows(TURNED, (2,))
    pair_columns(0)
    mix_columns(1)
    mix_rows(3)
    send_rows(3)
    mix_columns(2)
    pair_columns(1)
    mix_columns(3)
    pair_columns(2)
    pair_columns(3)
    reduce_x(0)
    reduce_x(2)
    reduce_columns(0)
    reduce_x(3)
    turned_zh()
    reduce_columns(1)
    reduce_zh(0)
    reduce_columns(2)
    reduce_zh(2)
    reduce_columns(3)
    turned_x()
    reduce_zh(3)

    def product(first, second):
        return jnp.dot(first, second, preferred_element_type=F32)

    full = None
    for chunk in (0, 2, 1, 3):
        arrived(ball.at[pl.ds(0, 3), chunk], b3r.at[chunk])
        right_high, right_low = split(jnp.concatenate(
            [ball[:, chunk, :, half * 16 : (half + 1) * 16].reshape(128, 128) for half in range(2)],
            axis=0,
        ))
        arrived(aall.at[pl.ds(0, 7), chunk], yr.at[chunk])
        left = aall[:, chunk].reshape(128, 128).T
        left_high, left_low = split(jnp.concatenate([left[:64], left[64:]], axis=1))
        if chunk == LAST:
            break
        term = (
            product(left_high, right_high)
            + product(left_high, right_low)
            + product(left_low, right_high)
        )
        full = term if full is None else full + term
    for part in range(2):
        rows = slice(part * 32, (part + 1) * 32)
        term = (
            product(left_high[rows], right_high)
            + product(left_high[rows], right_low)
            + product(left_low[rows], right_high)
        )
        psend[rows] = full[rows] + term
        send(psend.at[rows], precv.at[rows], pr.at[part], other_seq)
    for part in range(2):
        rows = slice(part * 32, (part + 1) * 32)
        arrived(precv.at[rows], pr.at[part])
        out[0, rows] = psend[rows] + precv[rows]
    arrived(sizes, sent)


def body(out_grads, layer_inputs, row_bits, col_bits, row_blocks, col_blocks):
    vmem = pl.BlockSpec(memory_space=pltpu.VMEM)
    hbm = pl.BlockSpec(memory_space=pl.ANY)
    dma = pltpu.SemaphoreType.DMA
    return pl.pallas_call(
        kernel,
        out_shape=pltpu.VMEM((1, 64, 128), F32),
        in_specs=[hbm] * 6,
        out_specs=vmem,
        scratch_shapes=[
            pltpu.SMEM((16,), jnp.int32),
            pltpu.SMEM((8,), jnp.int32),
            pltpu.VMEM((16, 128), jnp.int32),
            pltpu.VMEM((8, 128), jnp.int32),
            pltpu.VMEM((CHUNKS, 32, 2048), BF16),
            pltpu.VMEM((CHUNKS, 2, 32, 1024), BF16),
            pltpu.VMEM((256, 256), BF16),
            pltpu.VMEM((16, 32, 128), F32),
            pltpu.VMEM((8, 64, 128), F32),
            pltpu.VMEM((CHUNKS, 16, 16, 128), F32),
            pltpu.VMEM((CHUNKS, 3, 4, 16, 128), F32),
            pltpu.VMEM((CHUNKS, 4, 16, 128), F32),
            pltpu.VMEM((CHUNKS, 3, 16, 128), F32),
            pltpu.VMEM((8, CHUNKS, 16, 128), F32),
            pltpu.VMEM((3, 4, 16, 128), F32),
            pltpu.VMEM((4, 16, 128), F32),
            pltpu.VMEM((3, 16, 128), F32),
            pltpu.VMEM((CHUNKS, 2, 4, 2, 32, 128), F32),
            pltpu.VMEM((CHUNKS, 4, 2, 32, 128), F32),
            pltpu.VMEM((CHUNKS, 4, 2, 32, 128), F32),
            pltpu.VMEM((CHUNKS, 3, 2, 32, 128), F32),
            pltpu.VMEM((4, 4, 2, 32, 128), F32),
            pltpu.VMEM((64, 128), F32),
            pltpu.VMEM((64, 128), F32),
            dma((2,)), dma(()), dma((4,)), dma(()),
            dma((CHUNKS,)), dma((CHUNKS,)), dma((CHUNKS,)),
            dma((CHUNKS,)), dma((CHUNKS,)), dma((CHUNKS,)),
            dma((2,)),
            pltpu.SemaphoreType.REGULAR,
            pltpu.VMEM((SENT // 512, 128), F32),
        ],
        compiler_params=pltpu.CompilerParams(collective_id=0, has_side_effects=True),
        name="sketch",
    )(
        row_blocks, col_blocks, row_bits.reshape(16, 128), col_bits.reshape(8, 128),
        out_grads, layer_inputs,
    )


def solution(mesh):
    in_specs = (P(None, "seq", "row"), P(None, "seq", "col"), P("row"), P("col"), P(), P())
    out_specs = P(None, "row", "col")
    return jax.shard_map(body, mesh=mesh, in_specs=in_specs, out_specs=out_specs, check_vma=False)
```

```python
import math

import jax
import jax.numpy as jnp
from jax import lax
from jax.experimental import pallas as pl
from jax.experimental.pallas import tpu as pltpu
from jax.sharding import PartitionSpec as P

D = 8192
FF = 28672
FFP = 32768
SCALE = 1.0 / math.sqrt(FFP * D)
MESH = pl.DeviceIdType.MESH
CHUNKS = 4
TURNED = 1
LAST = 3
ROW_TILE, COL_TILE = 16 * 128 * 4, 64 * 128 * 4
SENT = (
    3 * 3 * 4 * ROW_TILE + 3 * 4 * ROW_TILE + 3 * 3 * ROW_TILE + 3 * ROW_TILE + CHUNKS * 7 * ROW_TILE
    + CHUNKS * 4 * COL_TILE + CHUNKS * 3 * COL_TILE + CHUNKS * 3 * COL_TILE + COL_TILE
)
F32 = jnp.float32
BF16 = jnp.bfloat16


def parity(value):
    value = value ^ (value >> 4)
    value = value ^ (value >> 2)
    value = value ^ (value >> 1)
    return value & 1


def parity_of_four(value):
    value = value ^ (value >> 2)
    value = value ^ (value >> 1)
    return value & 1


def butterfly(parts):
    stride = 1
    while stride < len(parts):
        for at in range(len(parts)):
            if not at & stride:
                low, high = parts[at], parts[at + stride]
                parts[at], parts[at + stride] = low + high, low - high
        stride *= 2
    return parts


def split(value):
    high = value.astype(BF16)
    return high, (value - high.astype(F32)).astype(BF16)


def kernel(
    row_blocks_in, col_blocks_in, row_bits_in, col_bits_in, grads, inputs, out,
    row_blocks, col_blocks, row_bits, col_bits,
    xbuf, ybuf, hmat, rmix, cmix, asend, xrecv, asum, zrecv, aall,
    zturn, zsum, xturn, bsend, bpair, bsum, brecv, ball, psend, precv,
    load_x, load_y, load_s, sent, xr, zr, yr, b1r, b2r, b3r, pr, in_zh, sizes,
):
    row, col, seq = lax.axis_index("row"), lax.axis_index("col"), lax.axis_index("seq")
    x, zh = row // 4, row % 4
    y, core = col // 2, col % 2

    def at_x(step):
        return {"row": ((x + step) % 4) * 4 + zh}

    def at_zh(step):
        return {"row": x * 4 + (zh + step) % 4}

    def at_col(dy, dc):
        return {"col": ((y + dy) % 4) * 2 + (core + dc) % 2}

    other_seq = {"seq": 1 - seq}

    barrier = pltpu.get_barrier_semaphore()
    partners = [at_x(step) for step in (2, 1, 3)]
    partners += [at_col(step, flip) for step in (2, 1, 3) for flip in range(2)]
    partners += [at_zh(1), at_zh(3), at_col(0, 1), other_seq]
    for partner in partners:
        pl.semaphore_signal(barrier, inc=1, device_id=partner, device_id_type=MESH)

    small = [
        pltpu.make_async_copy(src, dst, load_s.at[at])
        for at, (src, dst) in enumerate((
            (row_bits_in, row_bits), (row_blocks_in, row_blocks),
            (col_bits_in, col_bits), (col_blocks_in, col_blocks),
        ))
    ]
    loads_x = []
    for chunk in range(CHUNKS):
        start = pl.multiple_of(col * 128 + chunk * 32, 32)
        loads_x.append(
            pltpu.make_async_copy(grads.at[0, pl.ds(start, 32)], xbuf.at[chunk], load_x.at[min(chunk, 1)])
        )
    loads_y = [
        pltpu.make_async_copy(
            inputs.at[0, pl.ds(pl.multiple_of((x * 2 + half) * 128 + chunk * 32, 32), 32)],
            ybuf.at[chunk, half], load_y,
        )
        for chunk in range(CHUNKS)
        for half in range(2)
    ]
    for load in loads_x[:1] + small[:2] + loads_x[1:2] + small[2:] + loads_y[:2] + loads_x[2:] + loads_y[2:]:
        load.start()

    def send(src, dst, recv_sem, device):
        pltpu.make_async_remote_copy(
            src_ref=src, dst_ref=dst, send_sem=sent, recv_sem=recv_sem,
            device_id=device, device_id_type=MESH,
        ).start()

    def arrived(ref, sem):
        pltpu.make_async_copy(ref, ref, sem).wait()

    first = lax.broadcasted_iota(jnp.int32, (256, 256), 0)
    second = lax.broadcasted_iota(jnp.int32, (256, 256), 1)
    hmat[...] = (1 - 2 * parity(first & second)).astype(F32).astype(BF16)
    lane_high = lax.broadcasted_iota(jnp.int32, (16, 128), 1) // 64
    low = lane_high == 0
    place = lax.broadcasted_iota(jnp.int32, (16, 128), 0) * 128
    place = place + lax.broadcasted_iota(jnp.int32, (16, 128), 1) + row * 2048
    small[0].wait()
    row_sign = jnp.where(place < FF, (1 - 2 * row_bits[...]).astype(F32), 0.0).astype(BF16)

    def mix_columns(chunk):
        if chunk == 0:
            arrived(ybuf, load_y)
        tiles = []
        for half in range(2):
            for group in range(4):
                sign = jnp.concatenate(
                    [col_sign[2 * group : 2 * group + 1], col_sign[2 * group + 1 : 2 * group + 2]], axis=1
                )
                tiles.append(ybuf[chunk, half, :, group * 256 : (group + 1) * 256] * sign)
        mixed = jnp.dot(jnp.concatenate(tiles, axis=0), hmat[...], preferred_element_type=F32)
        for half in range(2):
            for tile in range(2):
                parts = butterfly([
                    mixed[(half * 4 + g) * 32 : (half * 4 + g + 1) * 32, tile * 128 : (tile + 1) * 128]
                    for g in range(4)
                ])
                for g in range(4):
                    cmix[g * 2 + tile, half * 32 : (half + 1) * 32] = parts[g]
        for m in range(8):
            kept = cmix[col_slots[m]] * col_signs[m]
            bsend[chunk, m % 2, m // 2] = kept.reshape(2, 32, 128)
        send(bsend.at[chunk, 1 - core], bpair.at[chunk], b1r.at[chunk], at_col(0, 1))

    def pair_columns(chunk):
        arrived(bpair.at[chunk], b1r.at[chunk])
        bsum[chunk] = bsend[chunk, core] + bpair[chunk]
        for step in (2, 1, 3):
            send(bsum.at[chunk, (y + step) % 4], brecv.at[chunk, step - 1], b2r.at[chunk], at_col(step, 0))

    def reduce_columns(chunk):
        arrived(brecv.at[chunk], b2r.at[chunk])
        ball[x, chunk] = (bsum[chunk, y] + brecv[chunk, 0]) + (brecv[chunk, 1] + brecv[chunk, 2])
        for step in (2, 1, 3):
            send(ball.at[x, chunk], ball.at[x, chunk], b3r.at[chunk], at_x(step))

    row_slots, row_signs = [], []

    def mix_rows(chunk):
        if chunk == 0:
            arrived(xbuf.at[0], load_x.at[0])
            small[1].wait()
            row_slots.extend(row_blocks[k] % 32 for k in range(16))
            row_signs.extend(
                (1 - 2 * parity_of_four((row_blocks[k] // 32) & row)).astype(F32) * SCALE for k in range(16)
            )
        if chunk == 1:
            arrived(xbuf.at[pl.ds(1, CHUNKS - 1)], load_x.at[1])
        tiles = []
        for group in range(8):
            sign = jnp.concatenate(
                [row_sign[2 * group : 2 * group + 1], row_sign[2 * group + 1 : 2 * group + 2]], axis=1
            )
            tiles.append(xbuf[chunk, :, group * 256 : (group + 1) * 256] * sign)
        mixed = jnp.dot(jnp.concatenate(tiles, axis=0), hmat[...], preferred_element_type=F32)
        for tile in range(2):
            parts = butterfly(
                [mixed[g * 32 : (g + 1) * 32, tile * 128 : (tile + 1) * 128] for g in range(8)]
            )
            for g in range(8):
                rmix[g * 2 + tile] = parts[g]
        for k in range(16):
            kept = rmix[row_slots[k] // 2]
            above, below = kept[:16], kept[16:]
            straight = jnp.where(low, above, below)
            crossed = pltpu.roll(jnp.where(low, below, above), 64, 1)
            slot = k if chunk != TURNED else (k % 4) * 4 + k // 4
            asend[chunk, slot] = jnp.where((lane_high ^ (row_slots[k] % 2)) == 0, straight, crossed) * row_signs[k]

    def send_rows(chunk, steps=(2, 1, 3)):
        for step in steps:
            if chunk == TURNED:
                first_k = ((zh + step) % 4) * 4
                send(asend.at[chunk, pl.ds(first_k, 4)], zturn.at[step - 1], zr.at[TURNED], at_zh(step))
            else:
                first_k = ((x + step) % 4) * 4
                send(asend.at[chunk, pl.ds(first_k, 4)], xrecv.at[chunk, step - 1], xr.at[chunk], at_x(step))

    def reduce_x(chunk):
        arrived(xrecv.at[chunk], xr.at[chunk])
        own = asend[chunk, pl.ds(x * 4, 4)]
        asum[chunk] = (own + xrecv[chunk, 0]) + (xrecv[chunk, 1] + xrecv[chunk, 2])
        for step in (2, 1, 3):
            send(asum.at[chunk, (zh + step) % 4], zrecv.at[chunk, step - 1], zr.at[chunk], at_zh(step))

    def spread(chunk):
        for step in (2, 1, 3):
            for flip in range(2):
                send(aall.at[col, chunk], aall.at[col, chunk], yr.at[chunk], at_col(step, flip))
        send(aall.at[col, chunk], aall.at[col, chunk], yr.at[chunk], at_col(0, 1))

    def reduce_zh(chunk):
        arrived(zrecv.at[chunk], zr.at[chunk])
        aall[col, chunk] = (asum[chunk, zh] + zrecv[chunk, 0]) + (zrecv[chunk, 1] + zrecv[chunk, 2])
        spread(chunk)

    def turned_zh():
        arrived(zturn, zr.at[TURNED])
        own = asend[TURNED, pl.ds(zh * 4, 4)]
        zsum[...] = (own + zturn[0]) + (zturn[1] + zturn[2])
        for step in (2, 1, 3):
            send(zsum.at[(x + step) % 4], xturn.at[step - 1], xr.at[TURNED], at_x(step))

    def turned_x():
        arrived(xturn, xr.at[TURNED])
        aall[col, TURNED] = (zsum[x] + xturn[0]) + (xturn[1] + xturn[2])
        spread(TURNED)

    mix_rows(0)
    pl.semaphore_wait(barrier, len(partners))
    pl.semaphore_signal(in_zh, inc=1, device_id=at_zh(3), device_id_type=MESH)
    send_rows(0)
    for load in small[2:]:
        load.wait()
    col_sign = (1 - 2 * col_bits[...]).astype(F32).astype(BF16)
    col_slots = [col_blocks[m] % 8 for m in range(8)]
    col_signs = [(1 - 2 * parity_of_four((col_blocks[m] // 8) & col)).astype(F32) for m in range(8)]
    mix_columns(0)
    mix_rows(TURNED)
    send_rows(TURNED, (1, 3))
    mix_rows(2)
    send_rows(2)
    pl.semaphore_wait(in_zh, 1)
    send_rows(TURNED, (2,))
    pair_columns(0)
    mix_columns(1)
    mix_rows(3)
    send_rows(3)
    mix_columns(2)
    pair_columns(1)
    mix_columns(3)
    pair_columns(2)
    pair_columns(3)
    reduce_x(0)
    reduce_x(2)
    reduce_columns(0)
    reduce_x(3)
    turned_zh()
    reduce_columns(1)
    reduce_zh(0)
    reduce_columns(2)
    reduce_zh(2)
    reduce_columns(3)
    turned_x()
    reduce_zh(3)

    def product(first, second):
        return jnp.dot(first, second, preferred_element_type=F32)

    full = None
    for chunk in (0, 2, 1, 3):
        arrived(ball.at[pl.ds(0, 3), chunk], b3r.at[chunk])
        right_high, right_low = split(jnp.concatenate(
            [ball[:, chunk, :, half * 16 : (half + 1) * 16].reshape(128, 128) for half in range(2)],
            axis=0,
        ))
        arrived(aall.at[pl.ds(0, 7), chunk], yr.at[chunk])
        left = aall[:, chunk].reshape(128, 128).T
        left_high, left_low = split(jnp.concatenate([left[:64], left[64:]], axis=1))
        if chunk == LAST:
            break
        term = (
            product(left_high, right_high)
            + product(left_high, right_low)
            + product(left_low, right_high)
        )
        full = term if full is None else full + term
    for part in range(2):
        rows = slice(part * 32, (part + 1) * 32)
        term = (
            product(left_high[rows], right_high)
            + product(left_high[rows], right_low)
            + product(left_low[rows], right_high)
        )
        psend[rows] = full[rows] + term
        send(psend.at[rows], precv.at[rows], pr.at[part], other_seq)
    for part in range(2):
        rows = slice(part * 32, (part + 1) * 32)
        arrived(precv.at[rows], pr.at[part])
        out[0, rows] = psend[rows] + precv[rows]
    arrived(sizes, sent)


def body(out_grads, layer_inputs, row_bits, col_bits, row_blocks, col_blocks):
    vmem = pl.BlockSpec(memory_space=pltpu.VMEM)
    hbm = pl.BlockSpec(memory_space=pl.ANY)
    dma = pltpu.SemaphoreType.DMA
    return pl.pallas_call(
        kernel,
        out_shape=pltpu.VMEM((1, 64, 128), F32),
        in_specs=[hbm] * 6,
        out_specs=vmem,
        scratch_shapes=[
            pltpu.SMEM((16,), jnp.int32),
            pltpu.SMEM((8,), jnp.int32),
            pltpu.VMEM((16, 128), jnp.int32),
            pltpu.VMEM((8, 128), jnp.int32),
            pltpu.VMEM((CHUNKS, 32, 2048), BF16),
            pltpu.VMEM((CHUNKS, 2, 32, 1024), BF16),
            pltpu.VMEM((256, 256), BF16),
            pltpu.VMEM((16, 32, 128), F32),
            pltpu.VMEM((8, 64, 128), F32),
            pltpu.VMEM((CHUNKS, 16, 16, 128), F32),
            pltpu.VMEM((CHUNKS, 3, 4, 16, 128), F32),
            pltpu.VMEM((CHUNKS, 4, 16, 128), F32),
            pltpu.VMEM((CHUNKS, 3, 16, 128), F32),
            pltpu.VMEM((8, CHUNKS, 16, 128), F32),
            pltpu.VMEM((3, 4, 16, 128), F32),
            pltpu.VMEM((4, 16, 128), F32),
            pltpu.VMEM((3, 16, 128), F32),
            pltpu.VMEM((CHUNKS, 2, 4, 2, 32, 128), F32),
            pltpu.VMEM((CHUNKS, 4, 2, 32, 128), F32),
            pltpu.VMEM((CHUNKS, 4, 2, 32, 128), F32),
            pltpu.VMEM((CHUNKS, 3, 2, 32, 128), F32),
            pltpu.VMEM((4, 4, 2, 32, 128), F32),
            pltpu.VMEM((64, 128), F32),
            pltpu.VMEM((64, 128), F32),
            dma((2,)), dma(()), dma((4,)), dma(()),
            dma((CHUNKS,)), dma((CHUNKS,)), dma((CHUNKS,)),
            dma((CHUNKS,)), dma((CHUNKS,)), dma((CHUNKS,)),
            dma((2,)),
            pltpu.SemaphoreType.REGULAR,
            pltpu.VMEM((SENT // 512, 128), F32),
        ],
        compiler_params=pltpu.CompilerParams(collective_id=0, has_side_effects=True),
        name="sketch",
    )(
        row_blocks, col_blocks, row_bits.reshape(16, 128), col_bits.reshape(8, 128),
        out_grads, layer_inputs,
    )


def solution(mesh):
    in_specs = (P(None, "seq", "row"), P(None, "seq", "col"), P("row"), P("col"), P(), P())
    out_specs = P(None, "row", "col")
    return jax.shard_map(body, mesh=mesh, in_specs=in_specs, out_specs=out_specs, check_vma=False)
```

```python
import math

import jax
import jax.numpy as jnp
from jax import lax
from jax.experimental import pallas as pl
from jax.experimental.pallas import tpu as pltpu
from jax.sharding import PartitionSpec as P

D = 8192
FF = 28672
FFP = 32768
SCALE = 1.0 / math.sqrt(FFP * D)
MESH = pl.DeviceIdType.MESH
CHUNKS = 4
TURNED = 1
LAST = 3
ROW_TILE, COL_TILE = 16 * 128 * 4, 64 * 128 * 4
SENT = (
    3 * 3 * 4 * ROW_TILE + 3 * 4 * ROW_TILE + 3 * 3 * ROW_TILE + 3 * ROW_TILE + CHUNKS * 7 * ROW_TILE
    + CHUNKS * 4 * COL_TILE + CHUNKS * 3 * COL_TILE + CHUNKS * 3 * COL_TILE + COL_TILE
)
F32 = jnp.float32
BF16 = jnp.bfloat16


def parity(value):
    value = value ^ (value >> 4)
    value = value ^ (value >> 2)
    value = value ^ (value >> 1)
    return value & 1


def parity_of_four(value):
    value = value ^ (value >> 2)
    value = value ^ (value >> 1)
    return value & 1


def butterfly(parts):
    stride = 1
    while stride < len(parts):
        for at in range(len(parts)):
            if not at & stride:
                low, high = parts[at], parts[at + stride]
                parts[at], parts[at + stride] = low + high, low - high
        stride *= 2
    return parts


def split(value):
    high = value.astype(BF16)
    return high, (value - high.astype(F32)).astype(BF16)


def kernel(
    row_blocks_in, col_blocks_in, row_bits_in, col_bits_in, grads, inputs, out,
    row_blocks, col_blocks, row_bits, col_bits,
    xbuf, ybuf, hmat, rmix, cmix, asend, xrecv, asum, zrecv, aall,
    zturn, zsum, xturn, bsend, bpair, bsum, brecv, ball, psend, precv,
    load_x, load_y, load_s, sent, xr, zr, yr, b1r, b2r, b3r, pr, in_zh, sizes,
):
    row, col, seq = lax.axis_index("row"), lax.axis_index("col"), lax.axis_index("seq")
    x, zh = row // 4, row % 4
    y, core = col // 2, col % 2

    def at_x(step):
        return {"row": ((x + step) % 4) * 4 + zh}

    def at_zh(step):
        return {"row": x * 4 + (zh + step) % 4}

    def at_col(dy, dc):
        return {"col": ((y + dy) % 4) * 2 + (core + dc) % 2}

    other_seq = {"seq": 1 - seq}

    barrier = pltpu.get_barrier_semaphore()
    partners = [at_x(step) for step in (2, 1, 3)]
    partners += [at_col(step, flip) for step in (2, 1, 3) for flip in range(2)]
    partners += [at_zh(1), at_zh(3), at_col(0, 1), other_seq]
    for partner in partners:
        pl.semaphore_signal(barrier, inc=1, device_id=partner, device_id_type=MESH)

    small = [
        pltpu.make_async_copy(src, dst, load_s.at[at])
        for at, (src, dst) in enumerate((
            (row_bits_in, row_bits), (row_blocks_in, row_blocks),
            (col_bits_in, col_bits), (col_blocks_in, col_blocks),
        ))
    ]
    loads_x = []
    for chunk in range(CHUNKS):
        start = pl.multiple_of(col * 128 + chunk * 32, 32)
        loads_x.append(
            pltpu.make_async_copy(grads.at[0, pl.ds(start, 32)], xbuf.at[chunk], load_x.at[min(chunk, 1)])
        )
    loads_y = [
        pltpu.make_async_copy(
            inputs.at[0, pl.ds(pl.multiple_of((x * 2 + half) * 128 + chunk * 32, 32), 32)],
            ybuf.at[chunk, half], load_y,
        )
        for chunk in range(CHUNKS)
        for half in range(2)
    ]
    for load in loads_x[:1] + small[:2] + loads_x[1:2] + small[2:] + loads_y[:2] + loads_x[2:] + loads_y[2:]:
        load.start()

    def send(src, dst, recv_sem, device):
        pltpu.make_async_remote_copy(
            src_ref=src, dst_ref=dst, send_sem=sent, recv_sem=recv_sem,
            device_id=device, device_id_type=MESH,
        ).start()

    def arrived(ref, sem):
        pltpu.make_async_copy(ref, ref, sem).wait()

    first = lax.broadcasted_iota(jnp.int32, (256, 256), 0)
    second = lax.broadcasted_iota(jnp.int32, (256, 256), 1)
    hmat[...] = (1 - 2 * parity(first & second)).astype(F32).astype(BF16)
    lane_high = lax.broadcasted_iota(jnp.int32, (16, 128), 1) // 64
    low = lane_high == 0
    place = lax.broadcasted_iota(jnp.int32, (16, 128), 0) * 128
    place = place + lax.broadcasted_iota(jnp.int32, (16, 128), 1) + row * 2048
    small[0].wait()
    row_sign = jnp.where(place < FF, (1 - 2 * row_bits[...]).astype(F32), 0.0).astype(BF16)

    def mix_columns(chunk):
        if chunk == 0:
            arrived(ybuf, load_y)
        tiles = []
        for half in range(2):
            for group in range(4):
                sign = jnp.concatenate(
                    [col_sign[2 * group : 2 * group + 1], col_sign[2 * group + 1 : 2 * group + 2]], axis=1
                )
                tiles.append(ybuf[chunk, half, :, group * 256 : (group + 1) * 256] * sign)
        mixed = jnp.dot(jnp.concatenate(tiles, axis=0), hmat[...], preferred_element_type=F32)
        for half in range(2):
            for tile in range(2):
                parts = butterfly([
                    mixed[(half * 4 + g) * 32 : (half * 4 + g + 1) * 32, tile * 128 : (tile + 1) * 128]
                    for g in range(4)
                ])
                for g in range(4):
                    cmix[g * 2 + tile, half * 32 : (half + 1) * 32] = parts[g]
        for m in range(8):
            kept = cmix[col_slots[m]] * col_signs[m]
            bsend[chunk, m % 2, m // 2] = kept.reshape(2, 32, 128)
        send(bsend.at[chunk, 1 - core], bpair.at[chunk], b1r.at[chunk], at_col(0, 1))

    def pair_columns(chunk):
        arrived(bpair.at[chunk], b1r.at[chunk])
        bsum[chunk] = bsend[chunk, core] + bpair[chunk]
        for step in (2, 1, 3):
            send(bsum.at[chunk, (y + step) % 4], brecv.at[chunk, step - 1], b2r.at[chunk], at_col(step, 0))

    def reduce_columns(chunk):
        arrived(brecv.at[chunk], b2r.at[chunk])
        ball[x, chunk] = (bsum[chunk, y] + brecv[chunk, 0]) + (brecv[chunk, 1] + brecv[chunk, 2])
        for step in (2, 1, 3):
            send(ball.at[x, chunk], ball.at[x, chunk], b3r.at[chunk], at_x(step))

    row_slots, row_signs = [], []

    def mix_rows(chunk):
        if chunk == 0:
            arrived(xbuf.at[0], load_x.at[0])
            small[1].wait()
            row_slots.extend(row_blocks[k] % 32 for k in range(16))
            row_signs.extend(
                (1 - 2 * parity_of_four((row_blocks[k] // 32) & row)).astype(F32) * SCALE for k in range(16)
            )
        if chunk == 1:
            arrived(xbuf.at[pl.ds(1, CHUNKS - 1)], load_x.at[1])
        tiles = []
        for group in range(8):
            sign = jnp.concatenate(
                [row_sign[2 * group : 2 * group + 1], row_sign[2 * group + 1 : 2 * group + 2]], axis=1
            )
            tiles.append(xbuf[chunk, :, group * 256 : (group + 1) * 256] * sign)
        mixed = jnp.dot(jnp.concatenate(tiles, axis=0), hmat[...], preferred_element_type=F32)
        for tile in range(2):
            parts = butterfly(
                [mixed[g * 32 : (g + 1) * 32, tile * 128 : (tile + 1) * 128] for g in range(8)]
            )
            for g in range(8):
                rmix[g * 2 + tile] = parts[g]
        for k in range(16):
            kept = rmix[row_slots[k] // 2]
            above, below = kept[:16], kept[16:]
            straight = jnp.where(low, above, below)
            crossed = pltpu.roll(jnp.where(low, below, above), 64, 1)
            slot = k if chunk != TURNED else (k % 4) * 4 + k // 4
            asend[chunk, slot] = jnp.where((lane_high ^ (row_slots[k] % 2)) == 0, straight, crossed) * row_signs[k]

    def send_rows(chunk, steps=(2, 1, 3)):
        for step in steps:
            if chunk == TURNED:
                first_k = ((zh + step) % 4) * 4
                send(asend.at[chunk, pl.ds(first_k, 4)], zturn.at[step - 1], zr.at[TURNED], at_zh(step))
            else:
                first_k = ((x + step) % 4) * 4
                send(asend.at[chunk, pl.ds(first_k, 4)], xrecv.at[chunk, step - 1], xr.at[chunk], at_x(step))

    def reduce_x(chunk):
        arrived(xrecv.at[chunk], xr.at[chunk])
        own = asend[chunk, pl.ds(x * 4, 4)]
        asum[chunk] = (own + xrecv[chunk, 0]) + (xrecv[chunk, 1] + xrecv[chunk, 2])
        for step in (2, 1, 3):
            send(asum.at[chunk, (zh + step) % 4], zrecv.at[chunk, step - 1], zr.at[chunk], at_zh(step))

    def spread(chunk):
        for step in (2, 1, 3):
            for flip in range(2):
                send(aall.at[col, chunk], aall.at[col, chunk], yr.at[chunk], at_col(step, flip))
        send(aall.at[col, chunk], aall.at[col, chunk], yr.at[chunk], at_col(0, 1))

    def reduce_zh(chunk):
        arrived(zrecv.at[chunk], zr.at[chunk])
        aall[col, chunk] = (asum[chunk, zh] + zrecv[chunk, 0]) + (zrecv[chunk, 1] + zrecv[chunk, 2])
        spread(chunk)

    def turned_zh():
        arrived(zturn, zr.at[TURNED])
        own = asend[TURNED, pl.ds(zh * 4, 4)]
        zsum[...] = (own + zturn[0]) + (zturn[1] + zturn[2])
        for step in (2, 1, 3):
            send(zsum.at[(x + step) % 4], xturn.at[step - 1], xr.at[TURNED], at_x(step))

    def turned_x():
        arrived(xturn, xr.at[TURNED])
        aall[col, TURNED] = (zsum[x] + xturn[0]) + (xturn[1] + xturn[2])
        spread(TURNED)

    mix_rows(0)
    pl.semaphore_wait(barrier, len(partners))
    pl.semaphore_signal(in_zh, inc=1, device_id=at_zh(3), device_id_type=MESH)
    send_rows(0)
    for load in small[2:]:
        load.wait()
    col_sign = (1 - 2 * col_bits[...]).astype(F32).astype(BF16)
    col_slots = [col_blocks[m] % 8 for m in range(8)]
    col_signs = [(1 - 2 * parity_of_four((col_blocks[m] // 8) & col)).astype(F32) for m in range(8)]
    mix_columns(0)
    mix_rows(TURNED)
    send_rows(TURNED, (1, 3))
    mix_rows(2)
    send_rows(2)
    pl.semaphore_wait(in_zh, 1)
    send_rows(TURNED, (2,))
    pair_columns(0)
    mix_columns(1)
    mix_rows(3)
    send_rows(3)
    mix_columns(2)
    pair_columns(1)
    mix_columns(3)
    pair_columns(2)
    pair_columns(3)
    reduce_x(0)
    reduce_x(2)
    reduce_columns(0)
    reduce_x(3)
    turned_zh()
    reduce_columns(1)
    reduce_columns(2)
    reduce_zh(0)
    reduce_zh(2)
    turned_x()
    reduce_columns(3)
    reduce_zh(3)

    def product(first, second):
        return jnp.dot(first, second, preferred_element_type=F32)

    full = None
    for chunk in (0, 2, 1, 3):
        arrived(ball.at[pl.ds(0, 3), chunk], b3r.at[chunk])
        right_high, right_low = split(jnp.concatenate(
            [ball[:, chunk, :, half * 16 : (half + 1) * 16].reshape(128, 128) for half in range(2)],
            axis=0,
        ))
        arrived(aall.at[pl.ds(0, 7), chunk], yr.at[chunk])
        left = aall[:, chunk].reshape(128, 128).T
        left_high, left_low = split(jnp.concatenate([left[:64], left[64:]], axis=1))
        if chunk == LAST:
            break
        term = (
            product(left_high, right_high)
            + product(left_high, right_low)
            + product(left_low, right_high)
        )
        full = term if full is None else full + term
    for part in range(2):
        rows = slice(part * 32, (part + 1) * 32)
        term = (
            product(left_high[rows], right_high)
            + product(left_high[rows], right_low)
            + product(left_low[rows], right_high)
        )
        psend[rows] = full[rows] + term
        send(psend.at[rows], precv.at[rows], pr.at[part], other_seq)
    for part in range(2):
        rows = slice(part * 32, (part + 1) * 32)
        arrived(precv.at[rows], pr.at[part])
        out[0, rows] = psend[rows] + precv[rows]
    arrived(sizes, sent)


def body(out_grads, layer_inputs, row_bits, col_bits, row_blocks, col_blocks):
    vmem = pl.BlockSpec(memory_space=pltpu.VMEM)
    hbm = pl.BlockSpec(memory_space=pl.ANY)
    dma = pltpu.SemaphoreType.DMA
    return pl.pallas_call(
        kernel,
        out_shape=pltpu.VMEM((1, 64, 128), F32),
        in_specs=[hbm] * 6,
        out_specs=vmem,
        scratch_shapes=[
            pltpu.SMEM((16,), jnp.int32),
            pltpu.SMEM((8,), jnp.int32),
            pltpu.VMEM((16, 128), jnp.int32),
            pltpu.VMEM((8, 128), jnp.int32),
            pltpu.VMEM((CHUNKS, 32, 2048), BF16),
            pltpu.VMEM((CHUNKS, 2, 32, 1024), BF16),
            pltpu.VMEM((256, 256), BF16),
            pltpu.VMEM((16, 32, 128), F32),
            pltpu.VMEM((8, 64, 128), F32),
            pltpu.VMEM((CHUNKS, 16, 16, 128), F32),
            pltpu.VMEM((CHUNKS, 3, 4, 16, 128), F32),
            pltpu.VMEM((CHUNKS, 4, 16, 128), F32),
            pltpu.VMEM((CHUNKS, 3, 16, 128), F32),
            pltpu.VMEM((8, CHUNKS, 16, 128), F32),
            pltpu.VMEM((3, 4, 16, 128), F32),
            pltpu.VMEM((4, 16, 128), F32),
            pltpu.VMEM((3, 16, 128), F32),
            pltpu.VMEM((CHUNKS, 2, 4, 2, 32, 128), F32),
            pltpu.VMEM((CHUNKS, 4, 2, 32, 128), F32),
            pltpu.VMEM((CHUNKS, 4, 2, 32, 128), F32),
            pltpu.VMEM((CHUNKS, 3, 2, 32, 128), F32),
            pltpu.VMEM((4, 4, 2, 32, 128), F32),
            pltpu.VMEM((64, 128), F32),
            pltpu.VMEM((64, 128), F32),
            dma((2,)), dma(()), dma((4,)), dma(()),
            dma((CHUNKS,)), dma((CHUNKS,)), dma((CHUNKS,)),
            dma((CHUNKS,)), dma((CHUNKS,)), dma((CHUNKS,)),
            dma((2,)),
            pltpu.SemaphoreType.REGULAR,
            pltpu.VMEM((SENT // 512, 128), F32),
        ],
        compiler_params=pltpu.CompilerParams(collective_id=0, has_side_effects=True),
        name="sketch",
    )(
        row_blocks, col_blocks, row_bits.reshape(16, 128), col_bits.reshape(8, 128),
        out_grads, layer_inputs,
    )


def solution(mesh):
    in_specs = (P(None, "seq", "row"), P(None, "seq", "col"), P("row"), P("col"), P(), P())
    out_specs = P(None, "row", "col")
    return jax.shard_map(body, mesh=mesh, in_specs=in_specs, out_specs=out_specs, check_vma=False)
```

```python
import math

import jax
import jax.numpy as jnp
from jax import lax
from jax.experimental import pallas as pl
from jax.experimental.pallas import tpu as pltpu
from jax.sharding import PartitionSpec as P

D = 8192
FF = 28672
FFP = 32768
SCALE = 1.0 / math.sqrt(FFP * D)
MESH = pl.DeviceIdType.MESH
CHUNKS = 4
TURNED = 1
LAST = 3
ROW_TILE, COL_TILE = 16 * 128 * 4, 64 * 128 * 4
SENT = (
    3 * 3 * 4 * ROW_TILE + 3 * 4 * ROW_TILE + 3 * 3 * ROW_TILE + 3 * ROW_TILE + CHUNKS * 7 * ROW_TILE
    + CHUNKS * 4 * COL_TILE + CHUNKS * 3 * COL_TILE + CHUNKS * 3 * COL_TILE + COL_TILE
)
F32 = jnp.float32
BF16 = jnp.bfloat16


def parity(value):
    value = value ^ (value >> 4)
    value = value ^ (value >> 2)
    value = value ^ (value >> 1)
    return value & 1


def parity_of_four(value):
    value = value ^ (value >> 2)
    value = value ^ (value >> 1)
    return value & 1


def butterfly(parts):
    stride = 1
    while stride < len(parts):
        for at in range(len(parts)):
            if not at & stride:
                low, high = parts[at], parts[at + stride]
                parts[at], parts[at + stride] = low + high, low - high
        stride *= 2
    return parts


def split(value):
    high = value.astype(BF16)
    return high, (value - high.astype(F32)).astype(BF16)


def kernel(
    row_blocks_in, col_blocks_in, row_bits_in, col_bits_in, grads, inputs, out,
    row_blocks, col_blocks, row_bits, col_bits,
    xbuf, ybuf, hmat, rmix, cmix, asend, xrecv, asum, zrecv, aall,
    zturn, zsum, xturn, bsend, bpair, bsum, brecv, ball, psend, precv,
    load_x, load_y, load_s, sent, xr, zr, yr, b1r, b2r, b3r, pr, in_zh, sizes,
):
    row, col, seq = lax.axis_index("row"), lax.axis_index("col"), lax.axis_index("seq")
    x, zh = row // 4, row % 4
    y, core = col // 2, col % 2

    def at_x(step):
        return {"row": ((x + step) % 4) * 4 + zh}

    def at_zh(step):
        return {"row": x * 4 + (zh + step) % 4}

    def at_col(dy, dc):
        return {"col": ((y + dy) % 4) * 2 + (core + dc) % 2}

    other_seq = {"seq": 1 - seq}

    barrier = pltpu.get_barrier_semaphore()
    partners = [at_x(step) for step in (2, 1, 3)]
    partners += [at_col(step, flip) for step in (2, 1, 3) for flip in range(2)]
    partners += [at_zh(1), at_zh(3), at_col(0, 1), other_seq]
    for partner in partners:
        pl.semaphore_signal(barrier, inc=1, device_id=partner, device_id_type=MESH)

    small = [
        pltpu.make_async_copy(src, dst, load_s.at[at])
        for at, (src, dst) in enumerate((
            (row_bits_in, row_bits), (row_blocks_in, row_blocks),
            (col_bits_in, col_bits), (col_blocks_in, col_blocks),
        ))
    ]
    loads_x = []
    for chunk in range(CHUNKS):
        start = pl.multiple_of(col * 128 + chunk * 32, 32)
        loads_x.append(
            pltpu.make_async_copy(grads.at[0, pl.ds(start, 32)], xbuf.at[chunk], load_x.at[min(chunk, 1)])
        )
    loads_y = [
        pltpu.make_async_copy(
            inputs.at[0, pl.ds(pl.multiple_of((x * 2 + half) * 128 + chunk * 32, 32), 32)],
            ybuf.at[chunk, half], load_y,
        )
        for chunk in range(CHUNKS)
        for half in range(2)
    ]
    for load in loads_x[:1] + small[:2] + loads_x[1:2] + small[2:] + loads_y[:2] + loads_x[2:] + loads_y[2:]:
        load.start()

    def send(src, dst, recv_sem, device):
        pltpu.make_async_remote_copy(
            src_ref=src, dst_ref=dst, send_sem=sent, recv_sem=recv_sem,
            device_id=device, device_id_type=MESH,
        ).start()

    def arrived(ref, sem):
        pltpu.make_async_copy(ref, ref, sem).wait()

    first = lax.broadcasted_iota(jnp.int32, (256, 256), 0)
    second = lax.broadcasted_iota(jnp.int32, (256, 256), 1)
    hmat[...] = (1 - 2 * parity(first & second)).astype(F32).astype(BF16)
    lane_high = lax.broadcasted_iota(jnp.int32, (16, 128), 1) // 64
    low = lane_high == 0
    place = lax.broadcasted_iota(jnp.int32, (16, 128), 0) * 128
    place = place + lax.broadcasted_iota(jnp.int32, (16, 128), 1) + row * 2048
    small[0].wait()
    row_sign = jnp.where(place < FF, (1 - 2 * row_bits[...]).astype(F32), 0.0).astype(BF16)

    def mix_columns(chunk):
        if chunk == 0:
            arrived(ybuf, load_y)
        tiles = []
        for half in range(2):
            for group in range(4):
                sign = jnp.concatenate(
                    [col_sign[2 * group : 2 * group + 1], col_sign[2 * group + 1 : 2 * group + 2]], axis=1
                )
                tiles.append(ybuf[chunk, half, :, group * 256 : (group + 1) * 256] * sign)
        mixed = jnp.dot(jnp.concatenate(tiles, axis=0), hmat[...], preferred_element_type=F32)
        for half in range(2):
            for tile in range(2):
                parts = butterfly([
                    mixed[(half * 4 + g) * 32 : (half * 4 + g + 1) * 32, tile * 128 : (tile + 1) * 128]
                    for g in range(4)
                ])
                for g in range(4):
                    cmix[g * 2 + tile, half * 32 : (half + 1) * 32] = parts[g]
        for m in range(8):
            kept = cmix[col_slots[m]] * col_signs[m]
            bsend[chunk, m % 2, m // 2] = kept.reshape(2, 32, 128)
        send(bsend.at[chunk, 1 - core], bpair.at[chunk], b1r.at[chunk], at_col(0, 1))

    def pair_columns(chunk):
        arrived(bpair.at[chunk], b1r.at[chunk])
        bsum[chunk] = bsend[chunk, core] + bpair[chunk]
        for step in (2, 1, 3):
            send(bsum.at[chunk, (y + step) % 4], brecv.at[chunk, step - 1], b2r.at[chunk], at_col(step, 0))

    def reduce_columns(chunk):
        arrived(brecv.at[chunk], b2r.at[chunk])
        ball[x, chunk] = (bsum[chunk, y] + brecv[chunk, 0]) + (brecv[chunk, 1] + brecv[chunk, 2])
        for step in (2, 1, 3):
            send(ball.at[x, chunk], ball.at[x, chunk], b3r.at[chunk], at_x(step))

    row_slots, row_signs = [], []

    def mix_rows(chunk):
        if chunk == 0:
            arrived(xbuf.at[0], load_x.at[0])
            small[1].wait()
            row_slots.extend(row_blocks[k] % 32 for k in range(16))
            row_signs.extend(
                (1 - 2 * parity_of_four((row_blocks[k] // 32) & row)).astype(F32) * SCALE for k in range(16)
            )
        if chunk == 1:
            arrived(xbuf.at[pl.ds(1, CHUNKS - 1)], load_x.at[1])
        tiles = []
        for group in range(8):
            sign = jnp.concatenate(
                [row_sign[2 * group : 2 * group + 1], row_sign[2 * group + 1 : 2 * group + 2]], axis=1
            )
            tiles.append(xbuf[chunk, :, group * 256 : (group + 1) * 256] * sign)
        mixed = jnp.dot(jnp.concatenate(tiles, axis=0), hmat[...], preferred_element_type=F32)
        for tile in range(2):
            parts = butterfly(
                [mixed[g * 32 : (g + 1) * 32, tile * 128 : (tile + 1) * 128] for g in range(8)]
            )
            for g in range(8):
                rmix[g * 2 + tile] = parts[g]
        for k in range(16):
            kept = rmix[row_slots[k] // 2]
            above, below = kept[:16], kept[16:]
            straight = jnp.where(low, above, below)
            crossed = pltpu.roll(jnp.where(low, below, above), 64, 1)
            slot = k if chunk != TURNED else (k % 4) * 4 + k // 4
            asend[chunk, slot] = jnp.where((lane_high ^ (row_slots[k] % 2)) == 0, straight, crossed) * row_signs[k]

    def send_rows(chunk, steps=(2, 1, 3)):
        for step in steps:
            if chunk == TURNED:
                first_k = ((zh + step) % 4) * 4
                send(asend.at[chunk, pl.ds(first_k, 4)], zturn.at[step - 1], zr.at[TURNED], at_zh(step))
            else:
                first_k = ((x + step) % 4) * 4
                send(asend.at[chunk, pl.ds(first_k, 4)], xrecv.at[chunk, step - 1], xr.at[chunk], at_x(step))

    def reduce_x(chunk):
        arrived(xrecv.at[chunk], xr.at[chunk])
        own = asend[chunk, pl.ds(x * 4, 4)]
        asum[chunk] = (own + xrecv[chunk, 0]) + (xrecv[chunk, 1] + xrecv[chunk, 2])
        for step in (2, 1, 3):
            send(asum.at[chunk, (zh + step) % 4], zrecv.at[chunk, step - 1], zr.at[chunk], at_zh(step))

    def spread(chunk):
        for step, flip in ((2, 1), (2, 0), (1, 1), (3, 1), (1, 0), (3, 0), (0, 1)):
            send(aall.at[col, chunk], aall.at[col, chunk], yr.at[chunk], at_col(step, flip))

    def reduce_zh(chunk):
        arrived(zrecv.at[chunk], zr.at[chunk])
        aall[col, chunk] = (asum[chunk, zh] + zrecv[chunk, 0]) + (zrecv[chunk, 1] + zrecv[chunk, 2])
        spread(chunk)

    def turned_zh():
        arrived(zturn, zr.at[TURNED])
        own = asend[TURNED, pl.ds(zh * 4, 4)]
        zsum[...] = (own + zturn[0]) + (zturn[1] + zturn[2])
        for step in (2, 1, 3):
            send(zsum.at[(x + step) % 4], xturn.at[step - 1], xr.at[TURNED], at_x(step))

    def turned_x():
        arrived(xturn, xr.at[TURNED])
        aall[col, TURNED] = (zsum[x] + xturn[0]) + (xturn[1] + xturn[2])
        spread(TURNED)

    mix_rows(0)
    pl.semaphore_wait(barrier, len(partners))
    pl.semaphore_signal(in_zh, inc=1, device_id=at_zh(3), device_id_type=MESH)
    send_rows(0)
    for load in small[2:]:
        load.wait()
    col_sign = (1 - 2 * col_bits[...]).astype(F32).astype(BF16)
    col_slots = [col_blocks[m] % 8 for m in range(8)]
    col_signs = [(1 - 2 * parity_of_four((col_blocks[m] // 8) & col)).astype(F32) for m in range(8)]
    mix_columns(0)
    mix_rows(TURNED)
    send_rows(TURNED, (1, 3))
    mix_rows(2)
    send_rows(2)
    pl.semaphore_wait(in_zh, 1)
    send_rows(TURNED, (2,))
    pair_columns(0)
    mix_columns(1)
    mix_rows(3)
    send_rows(3)
    mix_columns(2)
    pair_columns(1)
    mix_columns(3)
    pair_columns(2)
    pair_columns(3)
    reduce_x(0)
    reduce_x(2)
    reduce_columns(0)
    reduce_x(3)
    turned_zh()
    reduce_columns(1)
    reduce_zh(0)
    reduce_columns(2)
    reduce_zh(2)
    reduce_columns(3)
    turned_x()
    reduce_zh(3)

    def product(first, second):
        return jnp.dot(first, second, preferred_element_type=F32)

    full = None
    for chunk in (0, 2, 1, 3):
        arrived(ball.at[pl.ds(0, 3), chunk], b3r.at[chunk])
        right_high, right_low = split(jnp.concatenate(
            [ball[:, chunk, :, half * 16 : (half + 1) * 16].reshape(128, 128) for half in range(2)],
            axis=0,
        ))
        arrived(aall.at[pl.ds(0, 7), chunk], yr.at[chunk])
        left = aall[:, chunk].reshape(128, 128).T
        left_high, left_low = split(jnp.concatenate([left[:64], left[64:]], axis=1))
        if chunk == LAST:
            break
        term = (
            product(left_high, right_high)
            + product(left_high, right_low)
            + product(left_low, right_high)
        )
        full = term if full is None else full + term
    for part in range(2):
        rows = slice(part * 32, (part + 1) * 32)
        term = (
            product(left_high[rows], right_high)
            + product(left_high[rows], right_low)
            + product(left_low[rows], right_high)
        )
        psend[rows] = full[rows] + term
        send(psend.at[rows], precv.at[rows], pr.at[part], other_seq)
    for part in range(2):
        rows = slice(part * 32, (part + 1) * 32)
        arrived(precv.at[rows], pr.at[part])
        out[0, rows] = psend[rows] + precv[rows]
    arrived(sizes, sent)


def body(out_grads, layer_inputs, row_bits, col_bits, row_blocks, col_blocks):
    vmem = pl.BlockSpec(memory_space=pltpu.VMEM)
    hbm = pl.BlockSpec(memory_space=pl.ANY)
    dma = pltpu.SemaphoreType.DMA
    return pl.pallas_call(
        kernel,
        out_shape=pltpu.VMEM((1, 64, 128), F32),
        in_specs=[hbm] * 6,
        out_specs=vmem,
        scratch_shapes=[
            pltpu.SMEM((16,), jnp.int32),
            pltpu.SMEM((8,), jnp.int32),
            pltpu.VMEM((16, 128), jnp.int32),
            pltpu.VMEM((8, 128), jnp.int32),
            pltpu.VMEM((CHUNKS, 32, 2048), BF16),
            pltpu.VMEM((CHUNKS, 2, 32, 1024), BF16),
            pltpu.VMEM((256, 256), BF16),
            pltpu.VMEM((16, 32, 128), F32),
            pltpu.VMEM((8, 64, 128), F32),
            pltpu.VMEM((CHUNKS, 16, 16, 128), F32),
            pltpu.VMEM((CHUNKS, 3, 4, 16, 128), F32),
            pltpu.VMEM((CHUNKS, 4, 16, 128), F32),
            pltpu.VMEM((CHUNKS, 3, 16, 128), F32),
            pltpu.VMEM((8, CHUNKS, 16, 128), F32),
            pltpu.VMEM((3, 4, 16, 128), F32),
            pltpu.VMEM((4, 16, 128), F32),
            pltpu.VMEM((3, 16, 128), F32),
            pltpu.VMEM((CHUNKS, 2, 4, 2, 32, 128), F32),
            pltpu.VMEM((CHUNKS, 4, 2, 32, 128), F32),
            pltpu.VMEM((CHUNKS, 4, 2, 32, 128), F32),
            pltpu.VMEM((CHUNKS, 3, 2, 32, 128), F32),
            pltpu.VMEM((4, 4, 2, 32, 128), F32),
            pltpu.VMEM((64, 128), F32),
            pltpu.VMEM((64, 128), F32),
            dma((2,)), dma(()), dma((4,)), dma(()),
            dma((CHUNKS,)), dma((CHUNKS,)), dma((CHUNKS,)),
            dma((CHUNKS,)), dma((CHUNKS,)), dma((CHUNKS,)),
            dma((2,)),
            pltpu.SemaphoreType.REGULAR,
            pltpu.VMEM((SENT // 512, 128), F32),
        ],
        compiler_params=pltpu.CompilerParams(collective_id=0, has_side_effects=True),
        name="sketch",
    )(
        row_blocks, col_blocks, row_bits.reshape(16, 128), col_bits.reshape(8, 128),
        out_grads, layer_inputs,
    )


def solution(mesh):
    in_specs = (P(None, "seq", "row"), P(None, "seq", "col"), P("row"), P("col"), P(), P())
    out_specs = P(None, "row", "col")
    return jax.shard_map(body, mesh=mesh, in_specs=in_specs, out_specs=out_specs, check_vma=False)
```

```python
import math

import jax
import jax.numpy as jnp
from jax import lax
from jax.experimental import pallas as pl
from jax.experimental.pallas import tpu as pltpu
from jax.sharding import PartitionSpec as P

D = 8192
FF = 28672
FFP = 32768
SCALE = 1.0 / math.sqrt(FFP * D)
MESH = pl.DeviceIdType.MESH
CHUNKS = 4
TURNED = 1
LAST = 3
ROW_TILE, COL_TILE = 16 * 128 * 4, 64 * 128 * 4
SENT = (
    3 * 3 * 4 * ROW_TILE + 3 * 4 * ROW_TILE + 3 * 3 * ROW_TILE + 3 * ROW_TILE + CHUNKS * 7 * ROW_TILE
    + CHUNKS * 4 * COL_TILE + CHUNKS * 3 * COL_TILE + CHUNKS * 3 * COL_TILE + COL_TILE
)
F32 = jnp.float32
BF16 = jnp.bfloat16


def parity(value):
    value = value ^ (value >> 4)
    value = value ^ (value >> 2)
    value = value ^ (value >> 1)
    return value & 1


def parity_of_four(value):
    value = value ^ (value >> 2)
    value = value ^ (value >> 1)
    return value & 1


def butterfly(parts):
    stride = 1
    while stride < len(parts):
        for at in range(len(parts)):
            if not at & stride:
                low, high = parts[at], parts[at + stride]
                parts[at], parts[at + stride] = low + high, low - high
        stride *= 2
    return parts


def split(value):
    high = value.astype(BF16)
    return high, (value - high.astype(F32)).astype(BF16)


def kernel(
    row_blocks_in, col_blocks_in, row_bits_in, col_bits_in, grads, inputs, out,
    row_blocks, col_blocks, row_bits, col_bits,
    xbuf, ybuf, hmat, rmix, cmix, asend, xrecv, asum, zrecv, aall,
    zturn, zsum, xturn, bsend, bpair, bsum, brecv, ball, psend, precv,
    load_x, load_y, load_s, sent, xr, zr, yr, b1r, b2r, b3r, pr, in_zh, sizes,
):
    row, col, seq = lax.axis_index("row"), lax.axis_index("col"), lax.axis_index("seq")
    x, zh = row // 4, row % 4
    y, core = col // 2, col % 2

    def at_x(step):
        return {"row": ((x + step) % 4) * 4 + zh}

    def at_zh(step):
        return {"row": x * 4 + (zh + step) % 4}

    def at_col(dy, dc):
        return {"col": ((y + dy) % 4) * 2 + (core + dc) % 2}

    other_seq = {"seq": 1 - seq}

    small = [
        pltpu.make_async_copy(src, dst, load_s.at[at])
        for at, (src, dst) in enumerate((
            (row_bits_in, row_bits), (row_blocks_in, row_blocks),
            (col_bits_in, col_bits), (col_blocks_in, col_blocks),
        ))
    ]
    loads_x = []
    for chunk in range(CHUNKS):
        start = pl.multiple_of(col * 128 + chunk * 32, 32)
        loads_x.append(
            pltpu.make_async_copy(grads.at[0, pl.ds(start, 32)], xbuf.at[chunk], load_x.at[min(chunk, 1)])
        )
    loads_y = [
        pltpu.make_async_copy(
            inputs.at[0, pl.ds(pl.multiple_of((x * 2 + half) * 128 + chunk * 32, 32), 32)],
            ybuf.at[chunk, half], load_y,
        )
        for chunk in range(CHUNKS)
        for half in range(2)
    ]
    loads_x[0].start()
    small[0].start()

    barrier = pltpu.get_barrier_semaphore()
    partners = [at_x(step) for step in (2, 1, 3)]
    partners += [at_col(step, flip) for step in (2, 1, 3) for flip in range(2)]
    partners += [at_zh(1), at_zh(3), at_col(0, 1), other_seq]
    for partner in partners:
        pl.semaphore_signal(barrier, inc=1, device_id=partner, device_id_type=MESH)

    for load in small[1:2] + loads_x[1:2] + small[2:] + loads_y[:2] + loads_x[2:] + loads_y[2:]:
        load.start()

    def send(src, dst, recv_sem, device):
        pltpu.make_async_remote_copy(
            src_ref=src, dst_ref=dst, send_sem=sent, recv_sem=recv_sem,
            device_id=device, device_id_type=MESH,
        ).start()

    def arrived(ref, sem):
        pltpu.make_async_copy(ref, ref, sem).wait()

    first = lax.broadcasted_iota(jnp.int32, (256, 256), 0)
    second = lax.broadcasted_iota(jnp.int32, (256, 256), 1)
    hmat[...] = (1 - 2 * parity(first & second)).astype(F32).astype(BF16)
    lane_high = lax.broadcasted_iota(jnp.int32, (16, 128), 1) // 64
    low = lane_high == 0
    place = lax.broadcasted_iota(jnp.int32, (16, 128), 0) * 128
    place = place + lax.broadcasted_iota(jnp.int32, (16, 128), 1) + row * 2048
    small[0].wait()
    row_sign = jnp.where(place < FF, (1 - 2 * row_bits[...]).astype(F32), 0.0).astype(BF16)

    def mix_columns(chunk):
        if chunk == 0:
            arrived(ybuf, load_y)
        tiles = []
        for half in range(2):
            for group in range(4):
                sign = jnp.concatenate(
                    [col_sign[2 * group : 2 * group + 1], col_sign[2 * group + 1 : 2 * group + 2]], axis=1
                )
                tiles.append(ybuf[chunk, half, :, group * 256 : (group + 1) * 256] * sign)
        mixed = jnp.dot(jnp.concatenate(tiles, axis=0), hmat[...], preferred_element_type=F32)
        for half in range(2):
            for tile in range(2):
                parts = butterfly([
                    mixed[(half * 4 + g) * 32 : (half * 4 + g + 1) * 32, tile * 128 : (tile + 1) * 128]
                    for g in range(4)
                ])
                for g in range(4):
                    cmix[g * 2 + tile, half * 32 : (half + 1) * 32] = parts[g]
        for m in range(8):
            kept = cmix[col_slots[m]] * col_signs[m]
            bsend[chunk, m % 2, m // 2] = kept.reshape(2, 32, 128)
        send(bsend.at[chunk, 1 - core], bpair.at[chunk], b1r.at[chunk], at_col(0, 1))

    def pair_columns(chunk):
        arrived(bpair.at[chunk], b1r.at[chunk])
        bsum[chunk] = bsend[chunk, core] + bpair[chunk]
        for step in (2, 1, 3):
            send(bsum.at[chunk, (y + step) % 4], brecv.at[chunk, step - 1], b2r.at[chunk], at_col(step, 0))

    def reduce_columns(chunk):
        arrived(brecv.at[chunk], b2r.at[chunk])
        ball[x, chunk] = (bsum[chunk, y] + brecv[chunk, 0]) + (brecv[chunk, 1] + brecv[chunk, 2])
        for step in (2, 1, 3):
            send(ball.at[x, chunk], ball.at[x, chunk], b3r.at[chunk], at_x(step))

    row_slots, row_signs = [], []

    def mix_rows(chunk):
        if chunk == 0:
            arrived(xbuf.at[0], load_x.at[0])
            small[1].wait()
            row_slots.extend(row_blocks[k] % 32 for k in range(16))
            row_signs.extend(
                (1 - 2 * parity_of_four((row_blocks[k] // 32) & row)).astype(F32) * SCALE for k in range(16)
            )
        if chunk == 1:
            arrived(xbuf.at[pl.ds(1, CHUNKS - 1)], load_x.at[1])
        tiles = []
        for group in range(8):
            sign = jnp.concatenate(
                [row_sign[2 * group : 2 * group + 1], row_sign[2 * group + 1 : 2 * group + 2]], axis=1
            )
            tiles.append(xbuf[chunk, :, group * 256 : (group + 1) * 256] * sign)
        mixed = jnp.dot(jnp.concatenate(tiles, axis=0), hmat[...], preferred_element_type=F32)
        for tile in range(2):
            parts = butterfly(
                [mixed[g * 32 : (g + 1) * 32, tile * 128 : (tile + 1) * 128] for g in range(8)]
            )
            for g in range(8):
                rmix[g * 2 + tile] = parts[g]
        for k in range(16):
            kept = rmix[row_slots[k] // 2]
            above, below = kept[:16], kept[16:]
            straight = jnp.where(low, above, below)
            crossed = pltpu.roll(jnp.where(low, below, above), 64, 1)
            slot = k if chunk != TURNED else (k % 4) * 4 + k // 4
            asend[chunk, slot] = jnp.where((lane_high ^ (row_slots[k] % 2)) == 0, straight, crossed) * row_signs[k]

    def send_rows(chunk, steps=(2, 1, 3)):
        for step in steps:
            if chunk == TURNED:
                first_k = ((zh + step) % 4) * 4
                send(asend.at[chunk, pl.ds(first_k, 4)], zturn.at[step - 1], zr.at[TURNED], at_zh(step))
            else:
                first_k = ((x + step) % 4) * 4
                send(asend.at[chunk, pl.ds(first_k, 4)], xrecv.at[chunk, step - 1], xr.at[chunk], at_x(step))

    def reduce_x(chunk):
        arrived(xrecv.at[chunk], xr.at[chunk])
        own = asend[chunk, pl.ds(x * 4, 4)]
        asum[chunk] = (own + xrecv[chunk, 0]) + (xrecv[chunk, 1] + xrecv[chunk, 2])
        for step in (2, 1, 3):
            send(asum.at[chunk, (zh + step) % 4], zrecv.at[chunk, step - 1], zr.at[chunk], at_zh(step))

    def spread(chunk):
        for step, flip in ((2, 1), (2, 0), (1, 1), (3, 1), (1, 0), (3, 0), (0, 1)):
            send(aall.at[col, chunk], aall.at[col, chunk], yr.at[chunk], at_col(step, flip))

    def reduce_zh(chunk):
        arrived(zrecv.at[chunk], zr.at[chunk])
        aall[col, chunk] = (asum[chunk, zh] + zrecv[chunk, 0]) + (zrecv[chunk, 1] + zrecv[chunk, 2])
        spread(chunk)

    def turned_zh():
        arrived(zturn, zr.at[TURNED])
        own = asend[TURNED, pl.ds(zh * 4, 4)]
        zsum[...] = (own + zturn[0]) + (zturn[1] + zturn[2])
        for step in (2, 1, 3):
            send(zsum.at[(x + step) % 4], xturn.at[step - 1], xr.at[TURNED], at_x(step))

    def turned_x():
        arrived(xturn, xr.at[TURNED])
        aall[col, TURNED] = (zsum[x] + xturn[0]) + (xturn[1] + xturn[2])
        spread(TURNED)

    mix_rows(0)
    pl.semaphore_wait(barrier, len(partners))
    pl.semaphore_signal(in_zh, inc=1, device_id=at_zh(3), device_id_type=MESH)
    send_rows(0)
    for load in small[2:]:
        load.wait()
    col_sign = (1 - 2 * col_bits[...]).astype(F32).astype(BF16)
    col_slots = [col_blocks[m] % 8 for m in range(8)]
    col_signs = [(1 - 2 * parity_of_four((col_blocks[m] // 8) & col)).astype(F32) for m in range(8)]
    mix_columns(0)
    mix_rows(TURNED)
    send_rows(TURNED, (1, 3))
    mix_rows(2)
    send_rows(2)
    pl.semaphore_wait(in_zh, 1)
    send_rows(TURNED, (2,))
    pair_columns(0)
    mix_columns(1)
    mix_rows(3)
    send_rows(3)
    mix_columns(2)
    pair_columns(1)
    mix_columns(3)
    pair_columns(2)
    pair_columns(3)
    reduce_x(0)
    reduce_x(2)
    reduce_columns(0)
    reduce_x(3)
    turned_zh()
    reduce_columns(1)
    reduce_zh(0)
    reduce_columns(2)
    reduce_zh(2)
    reduce_columns(3)
    turned_x()
    reduce_zh(3)

    def product(first, second):
        return jnp.dot(first, second, preferred_element_type=F32)

    full = None
    for chunk in (0, 2, 1, 3):
        arrived(ball.at[pl.ds(0, 3), chunk], b3r.at[chunk])
        right_high, right_low = split(jnp.concatenate(
            [ball[:, chunk, :, half * 16 : (half + 1) * 16].reshape(128, 128) for half in range(2)],
            axis=0,
        ))
        arrived(aall.at[pl.ds(0, 7), chunk], yr.at[chunk])
        left = aall[:, chunk].reshape(128, 128).T
        left_high, left_low = split(jnp.concatenate([left[:64], left[64:]], axis=1))
        if chunk == LAST:
            break
        term = (
            product(left_high, right_high)
            + product(left_high, right_low)
            + product(left_low, right_high)
        )
        full = term if full is None else full + term
    for part in range(2):
        rows = slice(part * 32, (part + 1) * 32)
        term = (
            product(left_high[rows], right_high)
            + product(left_high[rows], right_low)
            + product(left_low[rows], right_high)
        )
        psend[rows] = full[rows] + term
        send(psend.at[rows], precv.at[rows], pr.at[part], other_seq)
    for part in range(2):
        rows = slice(part * 32, (part + 1) * 32)
        arrived(precv.at[rows], pr.at[part])
        out[0, rows] = psend[rows] + precv[rows]
    arrived(sizes, sent)


def body(out_grads, layer_inputs, row_bits, col_bits, row_blocks, col_blocks):
    vmem = pl.BlockSpec(memory_space=pltpu.VMEM)
    hbm = pl.BlockSpec(memory_space=pl.ANY)
    dma = pltpu.SemaphoreType.DMA
    return pl.pallas_call(
        kernel,
        out_shape=pltpu.VMEM((1, 64, 128), F32),
        in_specs=[hbm] * 6,
        out_specs=vmem,
        scratch_shapes=[
            pltpu.SMEM((16,), jnp.int32),
            pltpu.SMEM((8,), jnp.int32),
            pltpu.VMEM((16, 128), jnp.int32),
            pltpu.VMEM((8, 128), jnp.int32),
            pltpu.VMEM((CHUNKS, 32, 2048), BF16),
            pltpu.VMEM((CHUNKS, 2, 32, 1024), BF16),
            pltpu.VMEM((256, 256), BF16),
            pltpu.VMEM((16, 32, 128), F32),
            pltpu.VMEM((8, 64, 128), F32),
            pltpu.VMEM((CHUNKS, 16, 16, 128), F32),
            pltpu.VMEM((CHUNKS, 3, 4, 16, 128), F32),
            pltpu.VMEM((CHUNKS, 4, 16, 128), F32),
            pltpu.VMEM((CHUNKS, 3, 16, 128), F32),
            pltpu.VMEM((8, CHUNKS, 16, 128), F32),
            pltpu.VMEM((3, 4, 16, 128), F32),
            pltpu.VMEM((4, 16, 128), F32),
            pltpu.VMEM((3, 16, 128), F32),
            pltpu.VMEM((CHUNKS, 2, 4, 2, 32, 128), F32),
            pltpu.VMEM((CHUNKS, 4, 2, 32, 128), F32),
            pltpu.VMEM((CHUNKS, 4, 2, 32, 128), F32),
            pltpu.VMEM((CHUNKS, 3, 2, 32, 128), F32),
            pltpu.VMEM((4, 4, 2, 32, 128), F32),
            pltpu.VMEM((64, 128), F32),
            pltpu.VMEM((64, 128), F32),
            dma((2,)), dma(()), dma((4,)), dma(()),
            dma((CHUNKS,)), dma((CHUNKS,)), dma((CHUNKS,)),
            dma((CHUNKS,)), dma((CHUNKS,)), dma((CHUNKS,)),
            dma((2,)),
            pltpu.SemaphoreType.REGULAR,
            pltpu.VMEM((SENT // 512, 128), F32),
        ],
        compiler_params=pltpu.CompilerParams(collective_id=0, has_side_effects=True),
        name="sketch",
    )(
        row_blocks, col_blocks, row_bits.reshape(16, 128), col_bits.reshape(8, 128),
        out_grads, layer_inputs,
    )


def solution(mesh):
    in_specs = (P(None, "seq", "row"), P(None, "seq", "col"), P("row"), P("col"), P(), P())
    out_specs = P(None, "row", "col")
    return jax.shard_map(body, mesh=mesh, in_specs=in_specs, out_specs=out_specs, check_vma=False)
```
